32 devices in a mesh: gx: 8 (over z, y), gy: 4 (over x, core).
Axes of the slice: x: 2, y: 2, z: 4, core: 2. Of those that a mesh axis runs over, the one named last changes fastest.
Arguments:
- cell_state: float32 [39, 65536], P(None, ('gx', 'gy')), may hold values from 0.1 to 2
- coupling: float32 [39, 39], replicated, may hold values from -1 to 1
- basal_rate: float32 [39], replicated, may hold values from 0.1 to 1
- half_sat: float32 [39], replicated, may hold values from 0.2 to 2
- decay_rate: float32 [39], replicated, may hold values from 0.1 to 1
- uptake_weight: float32 [39], replicated, may hold values from -1 to 1
- agent_counts: int32 [32], P(('gx', 'gy')), may hold values from 512 to 2048, as said below
- divider_ids: int32 [4096], P(('gx', 'gy')), may hold values from 0 to 2047, as said below
- destinations: int32 [4096, 1], P(('gx', 'gy')), may hold values from 0 to 7; in each aligned block of 128 rows (0 to 127, 128 to 255, ...) at most 32 rows name the same one
- voxel_index: int32 [65536], P(('gx', 'gy')), may hold values from 0 to 196607, as said below
- oxygen: float32 [64, 64, 512], P(None, 'gx', 'gy'), may hold values from 0.5 to 1.5
Outputs:
- new_state: float32 [39, 65536], P(None, ('gx', 'gy'))
- daughter_state: float32 [39, 8192], P(None, ('gx', 'gy'))
- new_oxygen: float32 [64, 64, 512], P(None, 'gx', 'gy')
The draws below stay inside these ranges and needn't reach their ends.
Inputs may be any that keep to these rules, and one draw needn't show every extreme that they name: Live agents of a device are its first agent_counts slots; at least 512, and some device holds 2048. `divider_ids`: each entry is below the live count of its device; entries may repeat. `destinations`: within the list of one device no x-slab is named by more than 32 rows. `voxel_index`: the named voxel lies in the agent's own x-slab or an adjacent one (s = 0, 1 or 2) and inside the grid, with y inside its device's range.
All inputs are finite; a program needn't handle non-finite values.
Results may differ from the reference program's by a relative error of at most 0.0011.
Values may be sent and summed in bfloat16 or wider, within the bound.
No kernel may reach another device: no remote copies, remote signals or barrier semaphores. Data moves between devices by JAX's collectives and lax.ppermute only.
A program may use at most 64 MiB of HBM per device.

```python
import math
import jax
import jax.numpy as jnp
import numpy as np
from jax import lax

SPECIES = 39
AG_DEV = 2048
DIV_DEV = 128
CX = 8
CY = 128
NZ = 64
CAP = 32
AGENTS = 65536
NX = 64
NY = 512
N_GX = 8
N_GY = 4


def count_table(key):
    base = jax.random.fold_in(key, 7001)
    devices = N_GX * N_GY
    counts = jax.random.randint(jax.random.fold_in(base, 1), (devices,), AG_DEV // 4, AG_DEV + 1)
    fullest = jax.random.randint(jax.random.fold_in(base, 2), (), 0, devices)
    return jnp.where(jnp.arange(devices) == fullest, AG_DEV, counts).astype(jnp.int32)


def draw_agent_counts(key, part):
    return count_table(key)


def draw_divider_ids(key, part):
    counts = count_table(key)
    devices = N_GX * N_GY
    raw_draw = jax.random.randint(jax.random.fold_in(key, 7003), (devices, DIV_DEV), 0, 1 << 20)
    return (raw_draw % counts[:, None]).reshape(-1).astype(jnp.int32)


def draw_voxel_index(key, part):
    devices = N_GX * N_GY
    owner_dev = jnp.arange(devices * AG_DEV, dtype=jnp.int32) // AG_DEV
    slab_x = owner_dev // N_GY
    offset = jax.random.randint(jax.random.fold_in(key, 7005), (devices * AG_DEV,), 0, 3)
    offset = jnp.where((slab_x == 0) & (offset == 0), 1, offset)
    offset = jnp.where((slab_x == N_GX - 1) & (offset == 2), 1, offset)
    inside = jax.random.randint(jax.random.fold_in(key, 7007), (devices * AG_DEV,), 0, NZ * CX * CY)
    return (offset * (NZ * CX * CY) + inside).astype(jnp.int32)


def levels(stream_key, extent, shards, least, high):
    factor_of, own = 1.0, jax.random.fold_in(stream_key, 6)
    for axis_at, shards_of in shards:
        heights = jnp.exp(jax.random.uniform(jax.random.fold_in(own, axis_at), (shards_of,), jnp.float32, least / len(shards), high / len(shards)))
        factor_of = factor_of * jnp.repeat(heights, extent[axis_at] // shards_of).reshape([-1 if axis == axis_at else 1 for axis in range(len(extent))])
    return factor_of


def deal_out(own_key, own, number, rows, count, top, most, slope):
    order = jax.random.permutation(own_key, count)
    crowded, usual = load_shares(count, rows * top, most, slope, True), load_shares(count, rows * top, most, slope, False)
    places = jnp.arange(count)

    def named(lengths, offset_by):
        used = int((lengths > 0).sum())
        fixed = max(1, used // 4)
        moved = fixed + (places - fixed + offset_by * (used - fixed)) % max(1, count - fixed)
        return jnp.zeros((count,), jnp.int32).at[order[jnp.where(places < fixed, places, moved)]].set(jnp.asarray(lengths, jnp.int32))

    lengths = jnp.where(number % 4 == 0, named(crowded, number // 4), named(usual, number - number // 4 - 1))
    mixed = jax.random.permutation(jax.random.fold_in(own, 3), count)
    donor, sink = mixed[0:count // 2 * 2:2], mixed[1:count // 2 * 2:2]
    margin = jnp.minimum(lengths[donor] - 1, most - lengths[sink]) // 2
    margin = jnp.where((donor == order[0]) | (sink == order[0]) | (lengths[sink] == 0), 0, jnp.maximum(margin, 0))
    moved = jax.random.randint(jax.random.fold_in(own, 4), (count // 2,), 0, 1 << 20) % (margin + 1)
    lengths = lengths.at[donor].add(-moved).at[sink].add(moved)
    items = jnp.searchsorted(jnp.cumsum(lengths), jnp.arange(rows * top), side="right").astype(jnp.int32)
    table = items.reshape(top, rows).T
    table = table[jax.random.permutation(jax.random.fold_in(own, 1), rows)]
    offset_by = jax.random.randint(jax.random.fold_in(own, 2), (rows, 1), 0, top)
    return jnp.take_along_axis(table, (jnp.arange(top)[None, :] + offset_by) % top, axis=1)


def load_shares(amount, total, most, lean, full):
    weights = [(1 << 20) // math.isqrt(grade ** lean) + 1 for grade in range(1, amount + 1)]
    largest = most if full else min(most, max(-(-total // amount), total * weights[0] // sum(weights)))
    least = 1 if total - largest >= amount - 1 else 0
    given, surplus = [largest] + [least] * (amount - 1), total - largest - least * (amount - 1)
    while surplus > 0:
        candidates = [i for i in range(1, amount) if given[i] < largest] or [i for i in range(1, amount) if given[i] < most]
        whole, budget = sum([weights[i] for i in candidates]), surplus
        for i in candidates:
            addition = min(most - given[i], max(1, budget * weights[i] // whole), surplus)
            given[i] = given[i] + addition
            surplus = surplus - addition
    return np.array(given)


def bell_draw(own_key, shape, scale, reach, kind=jnp.bfloat16):
    drawn = jax.random.normal(own_key, shape, jnp.float32) * scale
    return jnp.minimum(jnp.maximum(drawn, -reach), reach).astype(kind)


def setup_inputs(seed: int = 0) -> dict:
    arg_keys = jax.random.split(jax.random.key(seed), 12)
    cell_state = jnp.clip(0.1 + 1.9 * jax.random.uniform(arg_keys[0], (SPECIES, AGENTS), jnp.float32) ** levels(arg_keys[0], (SPECIES, AGENTS), ((1, 32),), -0.2, 0.2), 0.1, 2.0)
    coupling = bell_draw(arg_keys[1], (SPECIES, SPECIES), SPECIES ** -0.5, 1.0, jnp.float32)
    basal_rate = jnp.clip(jnp.exp(jax.random.uniform(arg_keys[2], (SPECIES,), jnp.float32, math.log(0.1), math.log(1.0))), 0.1, 1.0)
    half_sat = jnp.clip(jnp.exp(jax.random.uniform(arg_keys[3], (SPECIES,), jnp.float32, math.log(0.2), math.log(2.0))), 0.2, 2.0)
    decay_rate = jnp.clip(jnp.exp(jax.random.uniform(arg_keys[4], (SPECIES,), jnp.float32, math.log(0.1), math.log(1.0))), 0.1, 1.0)
    uptake_weight = bell_draw(arg_keys[5], (SPECIES,), SPECIES ** -0.5, 1.0, jnp.float32)
    agent_counts = draw_agent_counts(jax.random.fold_in(arg_keys[11], 71), 0)
    divider_ids = draw_divider_ids(jax.random.fold_in(arg_keys[11], 71), 0)
    destinations_keys = jax.random.split(jax.random.fold_in(arg_keys[8], 1), (N_GX * N_GY * DIV_DEV) // DIV_DEV)
    destinations_turns = jax.random.permutation(jax.random.fold_in(arg_keys[8], 3), (N_GX * N_GY * DIV_DEV) // DIV_DEV)
    destinations = jax.vmap(lambda own, number: deal_out(jax.random.fold_in(arg_keys[8], 2), own, number, DIV_DEV, N_GX, 1, CAP, 2))(destinations_keys, destinations_turns).reshape((N_GX * N_GY * DIV_DEV, 1))
    voxel_index = draw_voxel_index(jax.random.fold_in(arg_keys[11], 71), 0)
    oxygen = jnp.clip(0.5 + 1.0 * jax.random.uniform(arg_keys[10], (NZ, NX, NY), jnp.float32) ** levels(arg_keys[10], (NZ, NX, NY), ((1, 8), (2, 4)), -0.2, 0.2), 0.5, 1.5)
    return {"cell_state": cell_state, "coupling": coupling, "basal_rate": basal_rate, "half_sat": half_sat, "decay_rate": decay_rate, "uptake_weight": uptake_weight, "agent_counts": agent_counts, "divider_ids": divider_ids, "destinations": destinations, "voxel_index": voxel_index, "oxygen": oxygen}


time_step = 0.25
diffusion_number = 0.16


def network_rates(current, coupling, basal_rate, half_sat, decay_rate):
    square = current * current
    occupancy = square / (half_sat[:, None] * half_sat[:, None] + square)
    drive_sum = jnp.dot(coupling, occupancy, precision=lax.Precision.HIGHEST, preferred_element_type=jnp.float32)
    return basal_rate[:, None] + drive_sum - decay_rate[:, None] * current


def advance(current, coupling, basal_rate, half_sat, decay_rate):
    for substep in range(2):
        middle = current + (0.5 * time_step) * network_rates(current, coupling, basal_rate, half_sat, decay_rate)
        current = current + time_step * network_rates(middle, coupling, basal_rate, half_sat, decay_rate)
    return current


def diffuse(oxygen_field):
    padded = jnp.pad(oxygen_field, 1)
    beside = padded[2:, 1:-1, 1:-1] + padded[:-2, 1:-1, 1:-1]
    beside = beside + padded[1:-1, 2:, 1:-1] + padded[1:-1, :-2, 1:-1]
    beside = beside + padded[1:-1, 1:-1, 2:] + padded[1:-1, 1:-1, :-2]
    return oxygen_field + diffusion_number * (beside - 6.0 * oxygen_field)


def reference(cell_state, coupling, basal_rate, half_sat, decay_rate, uptake_weight, agent_counts, divider_ids, destinations, voxel_index, oxygen):
    devices = N_GX * N_GY
    new_state = advance(cell_state, coupling, basal_rate, half_sat, decay_rate)

    chosen = divider_ids.reshape(devices, DIV_DEV)
    target_slab = destinations.reshape(devices, DIV_DEV)
    grouped = cell_state.reshape(SPECIES, devices, AG_DEV)
    pick_index = jnp.broadcast_to(chosen[None], (SPECIES, devices, DIV_DEV))
    mothers = jnp.take_along_axis(grouped, pick_index, axis=2)
    matured = advance(mothers.reshape(SPECIES, devices * DIV_DEV), coupling, basal_rate, half_sat, decay_rate)
    matured = matured.reshape(SPECIES, devices, DIV_DEV)
    onehot = (target_slab[:, :, None] == jnp.arange(N_GX, dtype=jnp.int32)[None, None, :]).astype(jnp.int32)
    earlier = jnp.cumsum(onehot, axis=1) - onehot
    slot_rank = jnp.sum(earlier * onehot, axis=2)
    position = target_slab * CAP + slot_rank
    sender = jnp.broadcast_to(jnp.arange(devices, dtype=jnp.int32)[:, None], (devices, DIV_DEV))
    outgoing = jnp.zeros((SPECIES, devices, N_GX * CAP), jnp.float32).at[:, sender, position].set(matured)
    arranged = outgoing.reshape(SPECIES, N_GX, N_GY, N_GX, CAP).transpose(0, 3, 2, 1, 4)
    daughter_state = arranged.reshape(SPECIES, devices * N_GX * CAP)

    drive_sum = jnp.dot(uptake_weight, new_state, precision=lax.Precision.HIGHEST, preferred_element_type=jnp.float32)
    slot_all = jnp.arange(devices * AG_DEV, dtype=jnp.int32)
    local_rank = slot_all % AG_DEV
    owner_dev = slot_all // AG_DEV
    alive_mask = local_rank < agent_counts[owner_dev]
    uptake = jnp.where(alive_mask, jax.nn.softplus(drive_sum), 0.0).astype(jnp.bfloat16)
    uptake = lax.optimization_barrier(uptake).astype(jnp.float32)

    slab_x = owner_dev // N_GY
    slab_y = owner_dev % N_GY
    cell_y = voxel_index % CY
    flat_row = voxel_index // CY
    cell_x = flat_row % CX
    cell_z = (flat_row // CX) % NZ
    offset = flat_row // (CX * NZ)
    global_x = (slab_x + offset - 1) * CX + cell_x
    global_y = slab_y * CY + cell_y
    flat_voxel = (cell_z * (CX * N_GX) + global_x) * (CY * N_GY) + global_y
    deposit = jax.ops.segment_sum(uptake, flat_voxel, num_segments=NZ * CX * N_GX * CY * N_GY)
    oxygen_field = oxygen - deposit.reshape(NZ, CX * N_GX, CY * N_GY)
    for sweep_turn in range(4):
        oxygen_field = diffuse(oxygen_field)
    return new_state, daughter_state, oxygen_field
```

```python
import jax
import jax.numpy as jnp
from jax import lax
from jax.experimental import pallas as pl
from jax.experimental.pallas import tpu as pltpu
from jax.sharding import PartitionSpec as P

time_step = 0.25
diffusion_number = 0.16
sweeps = 4
GRID = ("gx", "gy")
LANES = 128
EXACT = lax.Precision.HIGHEST
f32, bf16, i32 = jnp.float32, jnp.bfloat16, jnp.int32
VMEM_LIMIT = 48 << 20


def full(shape):
    return pl.BlockSpec(shape, lambda: (0,) * len(shape))


def call(body, outs, name, inputs, smem=(), scratch=()):
    specs = [
        pl.BlockSpec(memory_space=pltpu.SMEM) if at in smem else full(value.shape)
        for at, value in enumerate(inputs)
    ]
    return pl.pallas_call(
        body,
        out_shape=tuple(jax.ShapeDtypeStruct(s, t) for s, t in outs),
        in_specs=specs,
        out_specs=tuple(full(s) for s, t in outs),
        scratch_shapes=scratch,
        compiler_params=pltpu.CompilerParams(vmem_limit_bytes=VMEM_LIMIT),
        name=name,
    )(*inputs)


def swap_pairs(grid_count, row_count, partner):
    pairs = []
    for g in range(grid_count):
        for h in range(row_count):
            p, q = partner(g, h)
            if not (0 <= p < grid_count and 0 <= q < row_count):
                p, q = g, h ^ 1
            pairs.append((g * row_count + h, p * row_count + q))
    return pairs


def near_even(g, h):
    return g ^ 1, h


def near_odd(g, h):
    return (g + 1 if g % 2 else g - 1), h


def far_even(g, h):
    return g ^ 2, h


def far_odd(g, h):
    return (g + 2 if g & 2 else g - 2), h


def side_even(g, h):
    return g, h ^ 1


def column(row, count):
    shape = (count, count)
    same = lax.broadcasted_iota(i32, shape, 0) == lax.broadcasted_iota(i32, shape, 1)
    return jnp.sum(jnp.where(same, jnp.broadcast_to(row, shape), 0), axis=1, keepdims=True)


def advance_kernel(
    count_ref, cell, coupling, basal, half, decay, weight, voxel, oxygen,
    new_state, message_even, message_odd, message_far, drive, *, cy, cx, nz,
):
    species, agents = cell.shape
    basal_c, half_c, decay_c, weight_c = (column(r[...], species) for r in (basal, half, decay, weight))
    half_square = half_c * half_c
    matrix = coupling[...]

    def rates(current):
        square = current * current
        occupancy = square / (half_square + square)
        product = jnp.dot(matrix, occupancy, precision=EXACT, preferred_element_type=f32)
        return basal_c + product - decay_c * current

    current = cell[...]
    for substep in range(2):
        middle = current + (0.5 * time_step) * rates(current)
        current = current + time_step * rates(middle)
    new_state[...] = current
    total = jnp.sum(weight_c * current, axis=0, keepdims=True)
    rows = agents // LANES
    for c in range(rows):
        drive[c : c + 1, :] = total[:, c * LANES : (c + 1) * LANES]
    x = drive[...]
    soft = jnp.maximum(x, 0.0) + jnp.log1p(jnp.exp(-jnp.abs(x)))
    slot = lax.broadcasted_iota(i32, (rows, LANES), 0) * LANES + lax.broadcasted_iota(i32, (rows, LANES), 1)
    uptake = jnp.where(slot < count_ref[0], soft, 0.0)
    code = voxel[...]
    at_y = code % cy
    at_x = (code // cy) % cx
    at_z = (code // (cy * cx)) % nz
    slab_x = (code // (cy * cx * nz)) * cx + at_x + cx // 2
    row = at_z * cx + slab_x % cx - nz * cx // 2
    col = (slab_x // cx) * cy + at_y - 2 * cy
    listing = jnp.concatenate([uptake, row.astype(f32), col.astype(f32)], axis=0).astype(bf16)
    own = oxygen[...] - 1.0
    turned = pltpu.roll(own, cx // 2, 1)
    low = lax.broadcasted_iota(i32, (nz // 2, cx, cy), 1) < cx // 2
    a, b = own[: nz // 2], own[nz // 2 :]
    ta, tb = turned[: nz // 2], turned[nz // 2 :]
    upper = jnp.where(low, ta, b)
    lower = jnp.where(low, a, tb)
    even = lax.axis_index("gx") % 2 == 0
    to_next = upper.reshape(nz // 2 * cx, cy)
    to_previous = lower.reshape(nz // 2 * cx, cy)
    head = nz // 2 * cx
    message_even[:head, :] = jnp.where(even, to_next, to_previous).astype(bf16)
    message_odd[:head, :] = jnp.where(even, to_previous, to_next).astype(bf16)
    message_even[head:, :] = listing
    message_odd[head:, :] = listing
    message_far[...] = listing


def deposit_kernel(
    oxygen, own_list, near_e, near_o, far_e, far_o, field, strips, strip_even, strip_odd,
    lists, total, *, grid_count,
):
    nz, cx, cy = oxygen.shape
    half = cx // 2
    head = nz // 2 * cx
    rows = own_list.shape[0] // 3
    g = lax.axis_index("gx")
    even = g % 2 == 0
    low_pair = g % 4 < 2
    has_next, has_previous = g + 1 < grid_count, g >= 1
    has_next2, has_previous2 = g + 2 < grid_count, g >= 2

    def keep(listing, valid):
        wide = listing.astype(f32)
        index = lax.broadcasted_iota(i32, wide.shape, 0)
        return jnp.where((index < rows) & jnp.logical_not(valid), 0.0, wide)

    e, o = near_e[...].astype(f32), near_o[...].astype(f32)
    after, before = jnp.where(even, e, o), jnp.where(even, o, e)
    fe, fo = far_e[...].astype(f32), far_o[...].astype(f32)
    lists[0] = own_list[...].astype(f32)
    lists[1] = keep(after[head:], has_next)
    lists[2] = keep(before[head:], has_previous)
    lists[3] = keep(jnp.where(low_pair, fe, fo), has_next2)
    lists[4] = keep(jnp.where(low_pair, fo, fe), has_previous2)
    chunk = 2 if rows % 2 == 0 else 1
    m = nz * cx
    row_at = (lax.broadcasted_iota(i32, (m, LANES), 0) - m // 2).astype(f32)
    col_at = lax.broadcasted_iota(i32, (2 * cy, LANES), 0).astype(f32)
    plan = ((0, -cy, 0, 2), (1, -2 * cy, 0, 2), (2, 0, 0, 2), (3, -2 * cy, 1, 2), (4, cy, 0, 1))
    total[...] = jnp.zeros_like(total)

    def block(turn, carry):
        for which, base, first, last in plan:
            width = (last - first) * cy
            lefts, rights = [], []
            for part in range(chunk):
                at = turn * chunk + part
                weight = lists[which, pl.ds(at, 1), :]
                row = lists[which, pl.ds(rows + at, 1), :]
                col = lists[which, pl.ds(2 * rows + at, 1), :]
                lefts.append(jnp.where(row_at == row, 1.0, 0.0).astype(bf16))
                rights.append(jnp.where(col_at[:width] + base == col, weight, 0.0).astype(bf16))
            left = jnp.concatenate(lefts, axis=1)
            right = jnp.concatenate(rights, axis=1)
            total[:, first * cy : last * cy] += lax.dot_general(
                left, right, (((1,), (1,)), ((), ())), preferred_element_type=f32
            )
        return carry

    lax.fori_loop(0, rows // chunk, block, 0)

    low = lax.broadcasted_iota(i32, (nz // 2, cx, cy), 1) < half
    inner = pltpu.roll(oxygen[...], half, 1)
    from_before = jnp.where(has_previous, before[:head] + 1.0, 0.0).reshape(nz // 2, cx, cy)
    from_after = jnp.where(has_next, after[:head] + 1.0, 0.0).reshape(nz // 2, cx, cy)
    before_b = pltpu.roll(from_before, half, 1)
    after_a, after_b = pltpu.roll(from_after, half, 1), from_after
    zh = nz // 2
    field[0, :zh] = jnp.where(low, from_before, inner[:zh]) - total[: head, :cy].reshape(zh, cx, cy)
    field[0, zh:] = jnp.where(low, before_b, inner[zh:]) - total[head:, :cy].reshape(zh, cx, cy)
    field[1, :zh] = jnp.where(low, inner[:zh], after_a) - total[: head, cy:].reshape(zh, cx, cy)
    field[1, zh:] = jnp.where(low, inner[zh:], after_b) - total[head:, cy:].reshape(zh, cx, cy)

    edge = 2 * sweeps
    picked = lax.broadcasted_iota(i32, (2 * edge, cy), 0)
    picked = jnp.where(picked < edge, picked, picked + cy - 2 * edge)
    picker = (picked == lax.broadcasted_iota(i32, (2 * edge, cy), 1)).astype(f32)
    for tile in range(2):
        flat = field[tile].reshape(m, cy)
        strips[:, tile * m : (tile + 1) * m] = lax.dot_general(
            picker, flat, (((1,), (1,)), ((), ())), precision=EXACT, preferred_element_type=f32
        )
    h_even = lax.axis_index("gy") % 2 == 0
    head_rows, tail_rows = strips[:sweeps, :], strips[2 * edge - sweeps :, :]
    strip_even[...] = jnp.where(h_even, tail_rows, head_rows)
    strip_odd[...] = jnp.where(h_even, head_rows, tail_rows)


def sweep_kernel(field, strips, got_even, got_odd, out, ping, pong, *, grid_count, row_count):
    two, nz, cx, cy = field.shape
    half = cx // 2
    m = nz * cx
    g, h = lax.axis_index("gx"), lax.axis_index("gy")
    h_even = h % 2 == 0
    keep_self = 1.0 - 6.0 * diffusion_number
    sub = lax.broadcasted_iota(i32, (cx, cy), 0)
    mask0 = jnp.where((g == 0) & (sub < half), 0.0, 1.0)
    mask1 = jnp.where((g == grid_count - 1) & (sub >= half), 0.0, 1.0)
    first_row, last_row = sub == 0, sub == cx - 1

    zero = jnp.zeros((cx, cy), f32)
    for buffer in (ping, pong):
        for tile in range(2):
            buffer[tile, 0] = zero
            buffer[tile, nz + 1] = zero
    ping[:, 1 : nz + 1] = field[...]

    def one_sweep(source, target):
        def plane(z, carry):
            c0, c1 = source[0, z], source[1, z]
            b0, b1 = source[0, z - 1] + source[0, z + 1], source[1, z - 1] + source[1, z + 1]
            d0, d1 = pltpu.roll(c0, cx - 1, 0), pltpu.roll(c1, cx - 1, 0)
            u0, u1 = pltpu.roll(c0, 1, 0), pltpu.roll(c1, 1, 0)
            b0 = b0 + jnp.where(last_row, d1, d0) + u0
            b1 = b1 + d1 + jnp.where(first_row, u0, u1)
            b0 = b0 + pltpu.roll(c0, 1, 1) + pltpu.roll(c0, cy - 1, 1)
            b1 = b1 + pltpu.roll(c1, 1, 1) + pltpu.roll(c1, cy - 1, 1)
            target[0, z] = (c0 + diffusion_number * (b0 - 6.0 * c0)) * mask0
            target[1, z] = (c1 + diffusion_number * (b1 - 6.0 * c1)) * mask1
            return carry

        lax.fori_loop(1, nz + 1, plane, 0, unroll=8)

    for turn in range(sweeps):
        one_sweep(*((ping, pong) if turn % 2 == 0 else (pong, ping)))
    main = ping if sweeps % 2 == 0 else pong

    edge = 2 * sweeps
    has_right, has_left = h + 1 < row_count, h >= 1
    a, b = got_even[...], got_odd[...]
    right = jnp.where(has_right, jnp.where(h_even, a, b), 0.0)
    left = jnp.where(has_left, jnp.where(h_even, b, a), 0.0)
    own = strips[...]
    band = jnp.concatenate([left, own, right], axis=0)
    count = band.shape[0]
    lane = lax.broadcasted_iota(i32, (count, m), 1)
    line = lax.broadcasted_iota(i32, (count, m), 0)
    outside = (line < sweeps) & jnp.logical_not(has_left) | (line >= count - sweeps) & jnp.logical_not(has_right)
    at_x = lane % cx
    on0 = jnp.where(outside | ((g == 0) & (at_x < half)), 0.0, 1.0)
    on1 = jnp.where(outside | ((g == grid_count - 1) & (at_x >= half)), 0.0, 1.0)
    x_first, x_last = at_x == 0, at_x == cx - 1
    z_first, z_last = lane < cx, lane >= m - cx
    s0, s1 = band[:, :m], band[:, m:]

    def beside(s):
        up = jnp.where(z_first, 0.0, pltpu.roll(s, cx, 1))
        down = jnp.where(z_last, 0.0, pltpu.roll(s, m - cx, 1))
        return up + down + pltpu.roll(s, 1, 0) + pltpu.roll(s, count - 1, 0)

    for turn in range(sweeps):
        n0 = jnp.where(x_last, pltpu.roll(s1, cx - 1, 1), pltpu.roll(s0, m - 1, 1)) + pltpu.roll(s0, 1, 1)
        n1 = pltpu.roll(s1, m - 1, 1) + jnp.where(x_first, pltpu.roll(s0, m - cx + 1, 1), pltpu.roll(s1, 1, 1))
        n0, n1 = n0 + beside(s0), n1 + beside(s1)
        s0 = (s0 + diffusion_number * (n0 - 6.0 * s0)) * on0
        s1 = (s1 + diffusion_number * (n1 - 6.0 * s1)) * on1
    mixed = jnp.where(at_x < half, s1, s0)
    final = jnp.concatenate([mixed[sweeps : 2 * sweeps], mixed[count - 2 * sweeps : count - sweeps]], axis=0)
    placed = lax.broadcasted_iota(i32, (edge, cy), 0)
    placed = jnp.where(placed < sweeps, placed, placed + cy - edge)
    placer = (placed == lax.broadcasted_iota(i32, (edge, cy), 1)).astype(f32)
    edges = lax.dot_general(
        final, placer, (((0,), (0,)), ((), ())), precision=EXACT, preferred_element_type=f32
    ).reshape(nz, cx, cy)
    shape = (nz, cx, cy)
    at_y = lax.broadcasted_iota(i32, shape, 2)
    low = lax.broadcasted_iota(i32, shape, 1) < half
    inside = jnp.where(low, main[1, 1 : nz + 1], main[0, 1 : nz + 1])
    merged = jnp.where((at_y < sweeps) | (at_y >= cy - sweeps), edges, inside)
    out[...] = pltpu.roll(merged, half, 1)


def pieces(value):
    high = value.astype(bf16)
    rest = value - high.astype(f32)
    middle = rest.astype(bf16)
    return high, middle, (rest - middle.astype(f32)).astype(bf16)


def part_shape(columns, capacity, step):
    return capacity * step


def first_send(buffer, mine, width):
    count = buffer.shape[1]
    half = count // 2
    left, right = buffer[:, :half], buffer[:, half:]
    if width == half:
        return jnp.where(mine, left, right)
    bit = (lax.broadcasted_iota(i32, left.shape, 1) // width) % 2 == 1
    moved = jnp.where(mine, pltpu.roll(right, width, 1), pltpu.roll(right, half - width, 1))
    return jnp.where(jnp.logical_xor(bit, mine), left, moved)


def take_in(buffer, got, mine, width):
    count = buffer.shape[1]
    half = count // 2
    left, right = buffer[:, :half], buffer[:, half:]
    if width == half:
        left, right = jnp.where(mine, got, left), jnp.where(mine, right, got)
    else:
        bit = (lax.broadcasted_iota(i32, left.shape, 1) // width) % 2 == 1
        other = jnp.logical_xor(bit, mine)
        moved = jnp.where(mine, pltpu.roll(got, half - width, 1), pltpu.roll(got, width, 1))
        left, right = jnp.where(other, moved, left), jnp.where(other, got, right)
    return jnp.concatenate([left, right], axis=1)


def daughter_kernel(state, ids, targets, buffer, send, *, capacity, step):
    species, agents = state.shape
    picks = ids.shape[1]
    columns = buffer.shape[1]
    target = targets[...]
    square = (picks, picks)
    across = jnp.broadcast_to(target, square)
    down = jnp.broadcast_to(column(target, picks), square)
    earlier = lax.broadcasted_iota(i32, square, 0) < lax.broadcasted_iota(i32, square, 1)
    rank = jnp.sum(jnp.where((across == down) & earlier, 1, 0), axis=0, keepdims=True)
    position = target * capacity + rank
    chosen = (lax.broadcasted_iota(i32, (agents, picks), 0) == ids[...]).astype(f32).astype(bf16)
    mothers = sum(jnp.dot(p, chosen, preferred_element_type=f32) for p in pieces(state[...]))
    placing = (lax.broadcasted_iota(i32, (columns, picks), 0) == position).astype(f32).astype(bf16)
    placed = sum(
        lax.dot_general(p, placing, (((1,), (1,)), ((), ())), preferred_element_type=f32)
        for p in pieces(mothers)
    )
    buffer[...] = placed
    mine = (lax.axis_index("gx") // step) % 2 == 1
    send[...] = first_send(placed, mine, capacity * step)


def relay_kernel(buffer, got, merged, *send, capacity, step, after):
    g = lax.axis_index("gx")
    value = take_in(buffer[...], got[...], (g // step) % 2 == 1, capacity * step)
    merged[...] = value
    if after:
        send[0][...] = first_send(value, (g // after) % 2 == 1, capacity * after)


def solution(mesh):
    grid_count, row_count = mesh.shape["gx"], mesh.shape["gy"]

    def swap(value, partner):
        return lax.ppermute(value, GRID, swap_pairs(grid_count, row_count, partner))

    def side_odd(g, h):
        p = h + 1 if h % 2 else h - 1
        return (g, p) if 0 <= p < row_count else (g, h ^ (row_count - 1))

    def shards(
        cell_state, coupling, basal_rate, half_sat, decay_rate, uptake_weight,
        agent_counts, divider_ids, destinations, voxel_index, oxygen,
    ):
        species, agents = cell_state.shape
        nz, cx, cy = oxygen.shape
        picks = divider_ids.shape[0]
        rows = agents // LANES
        head = nz // 2 * cx
        capacity = max(2, 2 * picks // grid_count)
        columns = grid_count * capacity

        def line(value):
            return value.reshape(1, -1)

        def kernel(body, **sizes):
            def run(*refs):
                return body(*refs, **sizes)

            return run

        new_state, message_even, message_odd, listing = call(
            kernel(advance_kernel, cy=cy, cx=cx, nz=nz),
            [((species, agents), f32), ((head + 3 * rows, LANES), bf16), ((head + 3 * rows, LANES), bf16),
             ((3 * rows, LANES), bf16)],
            "advance",
            [agent_counts, cell_state, coupling, line(basal_rate), line(half_sat), line(decay_rate),
             line(uptake_weight), voxel_index.reshape(rows, LANES), oxygen],
            smem=(0,),
            scratch=[pltpu.VMEM((rows, LANES), f32)],
        )
        near_e = swap(message_even, near_even)
        near_o = swap(message_odd, near_odd)
        far_e = swap(listing, far_even)
        far_o = swap(listing, far_odd)

        step = grid_count // 2
        buffer, send = call(
            kernel(daughter_kernel, capacity=capacity, step=step),
            [((species, columns), f32), ((species, columns // 2), f32)],
            "daughters",
            [new_state, line(divider_ids), line(destinations)],
        )

        m = nz * cx
        field, strips, strip_even, strip_odd = call(
            kernel(deposit_kernel, grid_count=grid_count),
            [((2, nz, cx, cy), f32), ((4 * sweeps, 2 * m), f32), ((sweeps, 2 * m), f32), ((sweeps, 2 * m), f32)],
            "deposit",
            [oxygen, listing, near_e, near_o, far_e, far_o],
            scratch=[pltpu.VMEM((5, 3 * rows, LANES), f32), pltpu.VMEM((m, 2 * cy), f32)],
        )
        got_even = swap(strip_even, side_even)
        got_odd = swap(strip_odd, side_odd)

        while step:
            after = step // 2
            got = swap(send, lambda g, h: (g ^ step, h))
            outs = [((species, columns), f32)] + ([((species, columns // 2), f32)] if after else [])
            result = call(kernel(relay_kernel, capacity=capacity, step=step, after=after), outs, "relay", [buffer, got])
            buffer = result[0]
            send = result[-1]
            step = after

        (new_oxygen,) = call(
            kernel(sweep_kernel, grid_count=grid_count, row_count=row_count),
            [((nz, cx, cy), f32)],
            "sweeps",
            [field, strips, got_even, got_odd],
            scratch=[pltpu.VMEM((2, nz + 2, cx, cy), f32), pltpu.VMEM((2, nz + 2, cx, cy), f32)],
        )
        return new_state, buffer, new_oxygen

    return jax.shard_map(
        shards,
        mesh=mesh,
        in_specs=(
            P(None, GRID), P(), P(), P(), P(), P(), P(GRID), P(GRID), P(GRID, None), P(GRID), P(None, "gx", "gy"),
        ),
        out_specs=(P(None, GRID), P(None, GRID), P(None, "gx", "gy")),
        check_vma=False,
    )
```

```python
import jax
import jax.numpy as jnp
from jax import lax
from jax.experimental import pallas as pl
from jax.experimental.pallas import tpu as pltpu
from jax.sharding import PartitionSpec as P

time_step = 0.25
diffusion_number = 0.16
sweeps = 4
GRID = ("gx", "gy")
LANES = 128
EXACT = lax.Precision.HIGHEST
f32, bf16, i32 = jnp.float32, jnp.bfloat16, jnp.int32
VMEM_LIMIT = 48 << 20


def call(body, outs, name, inputs, smem=(), hbm=(), scratch=(), cost=None):
    def spec(at, shape):
        if at in smem:
            return pl.BlockSpec(memory_space=pltpu.SMEM)
        return pl.BlockSpec(memory_space=pltpu.HBM) if at in hbm else pl.BlockSpec(memory_space=pltpu.VMEM)

    count = len(inputs)
    inputs = [pltpu.with_memory_space_constraint(v, pltpu.HBM) if at in hbm else v for at, v in enumerate(inputs)]
    return pl.pallas_call(
        body,
        out_shape=tuple(jax.ShapeDtypeStruct(s, t) for s, t in outs),
        in_specs=[spec(at, value.shape) for at, value in enumerate(inputs)],
        out_specs=tuple(spec(count + at, s) for at, (s, t) in enumerate(outs)),
        scratch_shapes=scratch,
        compiler_params=pltpu.CompilerParams(vmem_limit_bytes=VMEM_LIMIT),
        name=name,
    )(*inputs)


def swap_pairs(grid_count, row_count, partner):
    pairs = []
    for g in range(grid_count):
        for h in range(row_count):
            p, q = partner(g, h)
            if not (0 <= p < grid_count and 0 <= q < row_count):
                p, q = g, h ^ 1
            pairs.append((g * row_count + h, p * row_count + q))
    return pairs


def near_even(g, h):
    return g ^ 1, h


def near_odd(g, h):
    return (g + 1 if g % 2 else g - 1), h


def far_even(g, h):
    return g ^ 2, h


def far_odd(g, h):
    return (g + 2 if g & 2 else g - 2), h


def side_even(g, h):
    return g, h ^ 1


def column(row, count):
    shape = (count, count)
    same = lax.broadcasted_iota(i32, shape, 0) == lax.broadcasted_iota(i32, shape, 1)
    return jnp.sum(jnp.where(same, jnp.broadcast_to(row, shape), 0), axis=1, keepdims=True)


def advance_kernel(
    count_ref, cell_hbm, coupling_hbm, basal_hbm, half_hbm, decay_hbm, weight_hbm, voxel_hbm, oxygen_hbm,
    new_state, message_even, message_odd, message_far,
    cell, coupling, basal, half, decay, weight, voxel, oxygen, drive, semaphores, *, cy, cx, nz,
):
    pairs = (
        (cell_hbm, cell), (coupling_hbm, coupling), (basal_hbm, basal), (half_hbm, half), (decay_hbm, decay),
        (weight_hbm, weight), (voxel_hbm, voxel), (oxygen_hbm, oxygen),
    )
    copies = [pltpu.make_async_copy(a, b, semaphores.at[i]) for i, (a, b) in enumerate(pairs)]
    for copy in copies:
        copy.start()
    for copy in copies:
        copy.wait()
    species, agents = cell.shape
    basal_c, half_c, decay_c, weight_c = (column(r[...], species) for r in (basal, half, decay, weight))
    half_square = half_c * half_c
    matrix = coupling[...]

    def rates(current):
        square = current * current
        occupancy = square / (half_square + square)
        product = jnp.dot(matrix, occupancy, precision=EXACT, preferred_element_type=f32)
        return basal_c + product - decay_c * current

    current = cell[...]
    for substep in range(2):
        middle = current + (0.5 * time_step) * rates(current)
        current = current + time_step * rates(middle)
    new_state[...] = current
    total = jnp.sum(weight_c * current, axis=0, keepdims=True)
    rows = agents // LANES
    for c in range(rows):
        drive[c : c + 1, :] = total[:, c * LANES : (c + 1) * LANES]
    x = drive[...]
    soft = jnp.maximum(x, 0.0) + jnp.log1p(jnp.exp(-jnp.abs(x)))
    slot = lax.broadcasted_iota(i32, (rows, LANES), 0) * LANES + lax.broadcasted_iota(i32, (rows, LANES), 1)
    uptake = jnp.where(slot < count_ref[0], soft, 0.0)
    code = voxel[...]
    at_y = code % cy
    at_x = (code // cy) % cx
    at_z = (code // (cy * cx)) % nz
    slab_x = (code // (cy * cx * nz)) * cx + at_x + cx // 2
    row = at_z * cx + slab_x % cx - nz * cx // 2
    col = (slab_x // cx) * cy + at_y - 2 * cy
    listing = jnp.concatenate([uptake, row.astype(f32), col.astype(f32)], axis=0).astype(bf16)
    own = oxygen[...] - 1.0
    turned = pltpu.roll(own, cx // 2, 1)
    low = lax.broadcasted_iota(i32, (nz // 2, cx, cy), 1) < cx // 2
    a, b = own[: nz // 2], own[nz // 2 :]
    ta, tb = turned[: nz // 2], turned[nz // 2 :]
    upper = jnp.where(low, ta, b)
    lower = jnp.where(low, a, tb)
    even = lax.axis_index("gx") % 2 == 0
    to_next = upper.reshape(nz // 2 * cx, cy)
    to_previous = lower.reshape(nz // 2 * cx, cy)
    head = nz // 2 * cx
    message_even[:head, :] = jnp.where(even, to_next, to_previous).astype(bf16)
    message_odd[:head, :] = jnp.where(even, to_previous, to_next).astype(bf16)
    message_even[head:, :] = listing
    message_odd[head:, :] = listing
    message_far[...] = listing


def one_hots(lists, which, base, width, m, left, right, slot):
    rows = lists.shape[1] // 3
    pack = 16
    row_at = (lax.broadcasted_iota(i32, (m, LANES), 0) - m // 2).astype(f32).astype(bf16).reshape(m // pack, pack, LANES)
    col_at = (lax.broadcasted_iota(i32, (width, LANES), 0) + base).astype(f32).astype(bf16)
    col_at = col_at.reshape(width // pack, pack, LANES)
    one, zero = jnp.ones((), bf16), jnp.zeros((), bf16)

    def line(at):
        return jnp.broadcast_to(lists[which, at : at + 1, :], (pack, LANES)).astype(bf16)[None]

    for at in range(rows):
        columns = slice((slot * rows + at) * LANES, (slot * rows + at + 1) * LANES)
        hit = jnp.where(row_at == line(rows + at), one, zero)
        left[:, columns] = hit.reshape(m, LANES)
        spread = jnp.where(col_at == line(2 * rows + at), jnp.broadcast_to(line(at), col_at.shape), zero)
        right[:width, columns] = spread.reshape(width, LANES)


def product(left, right):
    return lax.dot_general(left, right, (((1,), (1,)), ((), ())), preferred_element_type=f32)


def own_kernel(oxygen_hbm, own_list, base, lists, left, right, oxygen, semaphore):
    copy = pltpu.make_async_copy(oxygen_hbm, oxygen, semaphore)
    copy.start()
    nz, cx, cy = oxygen.shape
    lists[0] = own_list[...].astype(f32)
    one_hots(lists, 0, -cy, 2 * cy, nz * cx, left, right, 0)
    total = product(left[...], right[...])
    copy.wait()
    low = lax.broadcasted_iota(i32, (nz, cx, cy), 1) < cx // 2
    inner = pltpu.roll(oxygen[...], cx // 2, 1)
    base[:, :cx, :] = jnp.where(low, 0.0, inner) - total[:, :cy].reshape(nz, cx, cy)
    base[:, cx:, :] = jnp.where(low, inner, 0.0) - total[:, cy:].reshape(nz, cx, cy)


def deposit_kernel(
    base, near_e, near_o, far_e, far_o, field, strips, strip_even, strip_odd,
    lists, left, right, far_left, far_right, *, grid_count,
):
    nz, cx, cy = base.shape[0], base.shape[1] // 2, base.shape[2]
    half, zh = cx // 2, nz // 2
    head = zh * cx
    m = nz * cx
    rows = far_e.shape[0] // 3
    g = lax.axis_index("gx")
    even = g % 2 == 0
    low_pair = g % 4 < 2
    has_next, has_previous = g + 1 < grid_count, g >= 1
    has_next2, has_previous2 = g + 2 < grid_count, g >= 2

    def keep(listing, valid):
        index = lax.broadcasted_iota(i32, listing.shape, 0)
        return jnp.where((index < rows) & jnp.logical_not(valid), 0.0, listing)

    e, o = near_e[...].astype(f32), near_o[...].astype(f32)
    after, before = jnp.where(even, e, o), jnp.where(even, o, e)
    fe, fo = far_e[...].astype(f32), far_o[...].astype(f32)
    lists[0] = keep(after[head:], has_next)
    lists[1] = keep(before[head:], has_previous)
    lists[2] = keep(jnp.where(low_pair, fe, fo), has_next2)
    lists[3] = keep(jnp.where(low_pair, fo, fe), has_previous2)
    one_hots(lists, 0, -2 * cy, 2 * cy, m, left, right, 0)
    one_hots(lists, 1, 0, 2 * cy, m, left, right, 1)
    total = product(left[...], right[...])
    one_hots(lists, 2, -2 * cy, cy, m, far_left, far_right, 0)
    total1 = total[:, cy:] + product(far_left[...], far_right[...])
    one_hots(lists, 3, cy, cy, m, far_left, far_right, 0)
    total0 = total[:, :cy] + product(far_left[...], far_right[...])

    low = lax.broadcasted_iota(i32, (zh, cx, cy), 1) < half
    from_before = jnp.where(has_previous, before[:head] + 1.0, 0.0).reshape(zh, cx, cy)
    from_after = jnp.where(has_next, after[:head] + 1.0, 0.0).reshape(zh, cx, cy)
    before_b = pltpu.roll(from_before, half, 1)
    after_a = pltpu.roll(from_after, half, 1)
    shape = (zh, cx, cy)
    field[:zh, :cx] = base[:zh, :cx] + jnp.where(low, from_before, 0.0) - total0[:head].reshape(shape)
    field[zh:, :cx] = base[zh:, :cx] + jnp.where(low, before_b, 0.0) - total0[head:].reshape(shape)
    field[:zh, cx:] = base[:zh, cx:] + jnp.where(low, 0.0, after_a) - total1[:head].reshape(shape)
    field[zh:, cx:] = base[zh:, cx:] + jnp.where(low, 0.0, from_after) - total1[head:].reshape(shape)

    edge = 2 * sweeps
    picked = lax.broadcasted_iota(i32, (2 * edge, cy), 0)
    picked = jnp.where(picked < edge, picked, picked + cy - 2 * edge)
    picker = (picked == lax.broadcasted_iota(i32, (2 * edge, cy), 1)).astype(f32).astype(bf16)
    flat = field[...].reshape(2 * m, cy)
    rims = sum(product(picker, piece) for piece in pieces(flat))
    strips[...] = rims
    h_even = lax.axis_index("gy") % 2 == 0
    head_rows, tail_rows = rims[:sweeps], rims[2 * edge - sweeps :]
    strip_even[...] = jnp.where(h_even, tail_rows, head_rows)
    strip_odd[...] = jnp.where(h_even, head_rows, tail_rows)


def sweep_kernel(field, out, ping, pong, *, grid_count):
    nz, width, cy = field.shape
    cx = width // 2
    g = lax.axis_index("gx")
    top = width
    sub = lax.broadcasted_iota(i32, (cx, cy), 0)
    masks = (
        jnp.where((g == 0) & (sub < cx // 2), 0.0, diffusion_number),
        jnp.where((g == grid_count - 1) & (sub >= cx // 2), 0.0, diffusion_number),
    )
    centre = 1.0 / diffusion_number - 6.0
    zero = jnp.zeros((width, cy), f32)
    for buffer in (ping, pong):
        buffer[:top, :] = zero
        buffer[top + nz * width : top + nz * width + width, :] = zero
    ping[top : top + nz * width, :] = field[...].reshape(nz * width, cy)

    def one_sweep(source, target):
        def plane(z, carry):
            for tile in range(2):
                at = (z + 1) * width + tile * cx
                c = source[pl.ds(at, cx), :]
                total = source[pl.ds(at - width, cx), :] + source[pl.ds(at + width, cx), :]
                total = total + (source[pl.ds(at - 1, cx), :] + source[pl.ds(at + 1, cx), :])
                total = total + (pltpu.roll(c, 1, 1) + pltpu.roll(c, cy - 1, 1))
                target[pl.ds(at, cx), :] = (total + centre * c) * masks[tile]
            return carry

        lax.fori_loop(0, nz, plane, 0, unroll=8)

    for turn in range(sweeps):
        one_sweep(*((ping, pong) if turn % 2 == 0 else (pong, ping)))
    main = ping if sweeps % 2 == 0 else pong
    for z in range(nz):
        out[z] = main[pl.ds((z + 1) * width + cx // 2, cx), :]


def strip_kernel(inside, strips, got_even, got_odd, out, *, grid_count, row_count):
    nz, cx, cy = inside.shape
    m = strips.shape[1]
    width = m // nz
    g, h = lax.axis_index("gx"), lax.axis_index("gy")
    h_even = h % 2 == 0
    edge = 2 * sweeps
    has_right, has_left = h + 1 < row_count, h >= 1
    a, b = got_even[...], got_odd[...]
    right = jnp.where(has_right, jnp.where(h_even, a, b), 0.0)
    left = jnp.where(has_left, jnp.where(h_even, b, a), 0.0)
    band = jnp.concatenate([left, strips[...], right], axis=0)
    count = band.shape[0]
    lane = lax.broadcasted_iota(i32, (count, m), 1)
    line = lax.broadcasted_iota(i32, (count, m), 0)
    outside = (line < sweeps) & jnp.logical_not(has_left) | (line >= count - sweeps) & jnp.logical_not(has_right)
    at_x = lane % width
    outside = outside | (g == 0) & (at_x < cx // 2) | (g == grid_count - 1) & (at_x >= width - cx // 2)
    keep = jnp.where(outside, 0.0, diffusion_number)
    z_first, z_last = lane < width, lane >= m - width
    centre = 1.0 / diffusion_number - 6.0
    for turn in range(sweeps):
        total = jnp.where(z_first, 0.0, pltpu.roll(band, width, 1)) + jnp.where(z_last, 0.0, pltpu.roll(band, m - width, 1))
        total = total + (pltpu.roll(band, 1, 0) + pltpu.roll(band, count - 1, 0))
        total = total + (pltpu.roll(band, 1, 1) + pltpu.roll(band, m - 1, 1))
        band = (total + centre * band) * keep
    final = jnp.concatenate([band[sweeps : 2 * sweeps], band[count - 2 * sweeps : count - sweeps]], axis=0)
    placed = lax.broadcasted_iota(i32, (edge, cy), 0)
    placed = jnp.where(placed < sweeps, placed, placed + cy - edge)
    placer = (placed == lax.broadcasted_iota(i32, (edge, cy), 1)).astype(f32)
    edges = lax.dot_general(
        final, placer, (((0,), (0,)), ((), ())), precision=EXACT, preferred_element_type=f32
    ).reshape(nz, width, cy)
    low = lax.broadcasted_iota(i32, (nz, cx, cy), 1) < cx // 2
    mixed = pltpu.roll(jnp.where(low, edges[:, cx:], edges[:, :cx]), cx // 2, 1)
    at_y = lax.broadcasted_iota(i32, (nz, cx, cy), 2)
    out[...] = jnp.where((at_y < sweeps) | (at_y >= cy - sweeps), mixed, inside[...])


def pieces(value):
    high = value.astype(bf16)
    rest = value - high.astype(f32)
    middle = rest.astype(bf16)
    return high, middle, (rest - middle.astype(f32)).astype(bf16)


def first_send(buffer, mine, width):
    count = buffer.shape[1]
    half = count // 2
    left, right = buffer[:, :half], buffer[:, half:]
    if width == half:
        return jnp.where(mine, left, right)
    bit = (lax.broadcasted_iota(i32, left.shape, 1) // width) % 2 == 1
    moved = jnp.where(mine, pltpu.roll(right, width, 1), pltpu.roll(right, half - width, 1))
    return jnp.where(jnp.logical_xor(bit, mine), left, moved)


def take_in(buffer, got, mine, width):
    count = buffer.shape[1]
    half = count // 2
    left, right = buffer[:, :half], buffer[:, half:]
    if width == half:
        left, right = jnp.where(mine, got, left), jnp.where(mine, right, got)
    else:
        bit = (lax.broadcasted_iota(i32, left.shape, 1) // width) % 2 == 1
        other = jnp.logical_xor(bit, mine)
        moved = jnp.where(mine, pltpu.roll(got, half - width, 1), pltpu.roll(got, width, 1))
        left, right = jnp.where(other, moved, left), jnp.where(other, got, right)
    return jnp.concatenate([left, right], axis=1)


def daughter_kernel(state, ids, targets, new_state, buffer, send, semaphore, *, capacity, step):
    copy = pltpu.make_async_copy(state, new_state, semaphore)
    copy.start()
    species, agents = state.shape
    picks = ids.shape[1]
    columns = buffer.shape[1]
    target = targets[...]
    square = (picks, picks)
    across = jnp.broadcast_to(target, square)
    down = jnp.broadcast_to(column(target, picks), square)
    earlier = lax.broadcasted_iota(i32, square, 0) < lax.broadcasted_iota(i32, square, 1)
    rank = jnp.sum(jnp.where((across == down) & earlier, 1, 0), axis=0, keepdims=True)
    position = target * capacity + rank
    chosen = (lax.broadcasted_iota(i32, (agents, picks), 0) == ids[...]).astype(f32).astype(bf16)
    mothers = sum(jnp.dot(p, chosen, preferred_element_type=f32) for p in pieces(state[...]))
    placing = (lax.broadcasted_iota(i32, (columns, picks), 0) == position).astype(f32).astype(bf16)
    placed = sum(
        lax.dot_general(p, placing, (((1,), (1,)), ((), ())), preferred_element_type=f32)
        for p in pieces(mothers)
    )
    buffer[...] = placed
    mine = (lax.axis_index("gx") // step) % 2 == 1
    send[...] = first_send(placed, mine, capacity * step)
    copy.wait()


def relay_kernel(buffer, got, merged, *send, capacity, step, after):
    g = lax.axis_index("gx")
    value = take_in(buffer[...], got[...], (g // step) % 2 == 1, capacity * step)
    merged[...] = value
    if after:
        send[0][...] = first_send(value, (g // after) % 2 == 1, capacity * after)


def solution(mesh):
    grid_count, row_count = mesh.shape["gx"], mesh.shape["gy"]

    def swap(value, partner):
        return lax.ppermute(value, GRID, swap_pairs(grid_count, row_count, partner))

    def side_odd(g, h):
        p = h + 1 if h % 2 else h - 1
        return (g, p) if 0 <= p < row_count else (g, h ^ (row_count - 1))

    def shards(
        cell_state, coupling, basal_rate, half_sat, decay_rate, uptake_weight,
        agent_counts, divider_ids, destinations, voxel_index, oxygen,
    ):
        species, agents = cell_state.shape
        nz, cx, cy = oxygen.shape
        picks = divider_ids.shape[0]
        rows = agents // LANES
        head = nz // 2 * cx
        capacity = max(2, 2 * picks // grid_count)
        columns = grid_count * capacity

        def line(value):
            return value.reshape(1, -1)

        def kernel(body, **sizes):
            def run(*refs):
                return body(*refs, **sizes)

            return run

        m = nz * cx
        state, message_even, message_odd, listing = call(
            kernel(advance_kernel, cy=cy, cx=cx, nz=nz),
            [((species, agents), f32), ((head + 3 * rows, LANES), bf16), ((head + 3 * rows, LANES), bf16),
             ((3 * rows, LANES), bf16)],
            "advance",
            [agent_counts, cell_state, coupling, line(basal_rate), line(half_sat), line(decay_rate),
             line(uptake_weight), voxel_index.reshape(rows, LANES), oxygen],
            smem=(0,),
            hbm=range(1, 9),
            scratch=[pltpu.VMEM((species, agents), f32), pltpu.VMEM((species, species), f32)]
            + [pltpu.VMEM((1, species), f32)] * 4
            + [pltpu.VMEM((rows, LANES), i32), pltpu.VMEM((nz, cx, cy), f32), pltpu.VMEM((rows, LANES), f32),
               pltpu.SemaphoreType.DMA((8,))],
        )
        near_e = swap(message_even, near_even)
        near_o = swap(message_odd, near_odd)
        far_e = swap(listing, far_even)
        far_o = swap(listing, far_odd)

        step = grid_count // 2
        new_state, buffer, send = call(
            kernel(daughter_kernel, capacity=capacity, step=step),
            [((species, agents), f32), ((species, columns), f32), ((species, columns // 2), f32)],
            "daughters",
            [state, line(divider_ids), line(destinations)],
            hbm=(3,),
            scratch=[pltpu.SemaphoreType.DMA],
        )
        (base,) = call(
            own_kernel,
            [((nz, 2 * cx, cy), f32)],
            "own",
            [oxygen, listing],
            hbm=(0,),
            scratch=[pltpu.VMEM((1, 3 * rows, LANES), f32), pltpu.VMEM((m, agents), bf16), pltpu.VMEM((2 * cy, agents), bf16),
                     pltpu.VMEM((nz, cx, cy), f32), pltpu.SemaphoreType.DMA],
        )
        field, strips, strip_even, strip_odd = call(
            kernel(deposit_kernel, grid_count=grid_count),
            [((nz, 2 * cx, cy), f32), ((4 * sweeps, 2 * m), f32), ((sweeps, 2 * m), f32), ((sweeps, 2 * m), f32)],
            "deposit",
            [base, near_e, near_o, far_e, far_o],
            scratch=[pltpu.VMEM((4, 3 * rows, LANES), f32), pltpu.VMEM((m, 2 * agents), bf16),
                     pltpu.VMEM((2 * cy, 2 * agents), bf16), pltpu.VMEM((m, agents), bf16), pltpu.VMEM((cy, agents), bf16)],
        )
        got_even = swap(strip_even, side_even)
        got_odd = swap(strip_odd, side_odd)
        reach = (nz + 2) * 2 * cx
        (inside,) = call(
            kernel(sweep_kernel, grid_count=grid_count),
            [((nz, cx, cy), f32)],
            "sweeps",
            [field],
            scratch=[pltpu.VMEM((reach, cy), f32), pltpu.VMEM((reach, cy), f32)],
        )
        (new_oxygen,) = call(
            kernel(strip_kernel, grid_count=grid_count, row_count=row_count),
            [((nz, cx, cy), f32)],
            "strips",
            [inside, strips, got_even, got_odd],
        )
        stages = [strips, inside]
        while step:
            after = step // 2
            got = swap(send, lambda g, h: (g ^ step, h))
            if stages:
                got, _ = lax.optimization_barrier((got, stages.pop(0)))
            outs = [((species, columns), f32)] + ([((species, columns // 2), f32)] if after else [])
            result = call(kernel(relay_kernel, capacity=capacity, step=step, after=after), outs, "relay", [buffer, got])
            buffer = result[0]
            send = result[-1]
            step = after
        return new_state, buffer, new_oxygen

    return jax.shard_map(
        shards,
        mesh=mesh,
        in_specs=(
            P(None, GRID), P(), P(), P(), P(), P(), P(GRID), P(GRID), P(GRID, None), P(GRID), P(None, "gx", "gy"),
        ),
        out_specs=(P(None, GRID), P(None, GRID), P(None, "gx", "gy")),
        check_vma=False,
    )
```

```python
import jax
import jax.numpy as jnp
from jax import lax
from jax.experimental import pallas as pl
from jax.experimental.pallas import tpu as pltpu
from jax.sharding import PartitionSpec as P

time_step = 0.25
diffusion_number = 0.16
sweeps = 4
GRID = ("gx", "gy")
LANES = 128
EXACT = lax.Precision.HIGHEST
f32, bf16, i32 = jnp.float32, jnp.bfloat16, jnp.int32
VMEM_LIMIT = 48 << 20


def call(body, outs, name, inputs, smem=(), hbm=(), scratch=(), cost=None):
    def spec(at, shape):
        if at in smem:
            return pl.BlockSpec(memory_space=pltpu.SMEM)
        return pl.BlockSpec(memory_space=pltpu.HBM) if at in hbm else pl.BlockSpec(memory_space=pltpu.VMEM)

    count = len(inputs)
    inputs = [pltpu.with_memory_space_constraint(v, pltpu.HBM) if at in hbm else v for at, v in enumerate(inputs)]
    return pl.pallas_call(
        body,
        out_shape=tuple(jax.ShapeDtypeStruct(s, t) for s, t in outs),
        in_specs=[spec(at, value.shape) for at, value in enumerate(inputs)],
        out_specs=tuple(spec(count + at, s) for at, (s, t) in enumerate(outs)),
        scratch_shapes=scratch,
        compiler_params=pltpu.CompilerParams(vmem_limit_bytes=VMEM_LIMIT),
        name=name,
    )(*inputs)


def swap_pairs(grid_count, row_count, partner):
    pairs = []
    for g in range(grid_count):
        for h in range(row_count):
            p, q = partner(g, h)
            if not (0 <= p < grid_count and 0 <= q < row_count):
                p, q = g, h ^ 1
            pairs.append((g * row_count + h, p * row_count + q))
    return pairs


def near_even(g, h):
    return g ^ 1, h


def near_odd(g, h):
    return (g + 1 if g % 2 else g - 1), h


def far_even(g, h):
    return g ^ 2, h


def far_odd(g, h):
    return (g + 2 if g & 2 else g - 2), h


def side_even(g, h):
    return g, h ^ 1


def column(row, count):
    shape = (count, count)
    same = lax.broadcasted_iota(i32, shape, 0) == lax.broadcasted_iota(i32, shape, 1)
    return jnp.sum(jnp.where(same, jnp.broadcast_to(row, shape), 0), axis=1, keepdims=True)


def advance_kernel(
    count_ref, cell_hbm, coupling_hbm, basal_hbm, half_hbm, decay_hbm, weight_hbm, voxel_hbm, oxygen_hbm, ids_hbm,
    targets_hbm, new_state, message_even, message_odd, message_far, buffer,
    cell, coupling, basal, half, decay, weight, voxel, oxygen, ids, targets, drive, semaphores, *, cy, cx, nz, capacity,
):
    pairs = (
        (cell_hbm, cell), (coupling_hbm, coupling), (basal_hbm, basal), (half_hbm, half), (decay_hbm, decay),
        (weight_hbm, weight), (voxel_hbm, voxel), (oxygen_hbm, oxygen), (ids_hbm, ids), (targets_hbm, targets),
    )
    copies = [pltpu.make_async_copy(a, b, semaphores.at[i]) for i, (a, b) in enumerate(pairs)]
    for copy in copies:
        copy.start()
    for copy in copies:
        copy.wait()
    species, agents = cell.shape
    basal_c, half_c, decay_c, weight_c = (column(r[...], species) for r in (basal, half, decay, weight))
    half_square = half_c * half_c
    matrix = coupling[...]

    def rates(current):
        square = current * current
        occupancy = square / (half_square + square)
        product = jnp.dot(matrix, occupancy, precision=EXACT, preferred_element_type=f32)
        return basal_c + product - decay_c * current

    current = cell[...]
    for substep in range(2):
        middle = current + (0.5 * time_step) * rates(current)
        current = current + time_step * rates(middle)
    new_state[...] = current
    total = jnp.sum(weight_c * current, axis=0, keepdims=True)
    rows = agents // LANES
    for c in range(rows):
        drive[c : c + 1, :] = total[:, c * LANES : (c + 1) * LANES]
    x = drive[...]
    soft = jnp.maximum(x, 0.0) + jnp.log1p(jnp.exp(-jnp.abs(x)))
    slot = lax.broadcasted_iota(i32, (rows, LANES), 0) * LANES + lax.broadcasted_iota(i32, (rows, LANES), 1)
    uptake = jnp.where(slot < count_ref[0], soft, 0.0)
    code = voxel[...]
    at_y = code % cy
    at_x = (code // cy) % cx
    at_z = (code // (cy * cx)) % nz
    slab_x = (code // (cy * cx * nz)) * cx + at_x + cx // 2
    row = at_z * cx + slab_x % cx - nz * cx // 2
    col = (slab_x // cx) * cy + at_y - 2 * cy
    listing = jnp.concatenate([uptake, row.astype(f32), col.astype(f32)], axis=0).astype(bf16)
    own = oxygen[...] - 1.0
    turned = pltpu.roll(own, cx // 2, 1)
    low = lax.broadcasted_iota(i32, (nz // 2, cx, cy), 1) < cx // 2
    a, b = own[: nz // 2], own[nz // 2 :]
    ta, tb = turned[: nz // 2], turned[nz // 2 :]
    upper = jnp.where(low, ta, b)
    lower = jnp.where(low, a, tb)
    even = lax.axis_index("gx") % 2 == 0
    to_next = upper.reshape(nz // 2 * cx, cy)
    to_previous = lower.reshape(nz // 2 * cx, cy)
    head = nz // 2 * cx
    message_even[:head, :] = jnp.where(even, to_next, to_previous).astype(bf16)
    message_odd[:head, :] = jnp.where(even, to_previous, to_next).astype(bf16)
    tail = head + 3 * rows
    message_even[head:tail, :] = listing
    message_odd[head:, :] = listing
    message_far[...] = listing
    placed = place_daughters(current, ids[...], targets[...], capacity, buffer.shape[1])
    buffer[...] = placed
    put_pieces(message_even, tail, first_send(placed, lax.axis_index("gx") % 2 == 1, capacity))


def one_hots(lists, which, first, m, base, width, left, right, slot):
    rows = lists.shape[1] // 3
    pack = 16
    row_at = (lax.broadcasted_iota(i32, (m, LANES), 0) + first).astype(f32).astype(bf16).reshape(m // pack, pack, LANES)
    col_at = (lax.broadcasted_iota(i32, (width, LANES), 0) + base).astype(f32).astype(bf16)
    col_at = col_at.reshape(width // pack, pack, LANES)
    one, zero = jnp.ones((), bf16), jnp.zeros((), bf16)

    def line(at):
        return jnp.broadcast_to(lists[which, at : at + 1, :], (pack, LANES)).astype(bf16)[None]

    for at in range(rows):
        columns = slice((slot * rows + at) * LANES, (slot * rows + at + 1) * LANES)
        hit = jnp.where(row_at == line(rows + at), one, zero)
        left[:, columns] = hit.reshape(m, LANES)
        spread = jnp.where(col_at == line(2 * rows + at), jnp.broadcast_to(line(at), col_at.shape), zero)
        right[:width, columns] = spread.reshape(width, LANES)


def product(left, right):
    return lax.dot_general(left, right, (((1,), (1,)), ((), ())), preferred_element_type=f32)


def own_kernel(oxygen_hbm, own_list, state, base, new_state, lists, left, right, oxygen, semaphores):
    copy = pltpu.make_async_copy(oxygen_hbm, oxygen, semaphores.at[0])
    copy.start()
    store = pltpu.make_async_copy(state, new_state, semaphores.at[1])
    store.start()
    nz, cx, cy = oxygen.shape
    m = nz * cx
    lists[0] = own_list[...].astype(f32)
    one_hots(lists, 0, -m // 2, m, -cy, 2 * cy, left, right, 0)
    total = product(left[...], right[...])
    copy.wait()
    low = lax.broadcasted_iota(i32, (nz, cx, cy), 1) < cx // 2
    inner = pltpu.roll(oxygen[...], cx // 2, 1)
    base[:, :cx, :] = jnp.where(low, 0.0, inner) - total[:, :cy].reshape(nz, cx, cy)
    base[:, cx:, :] = jnp.where(low, inner, 0.0) - total[:, cy:].reshape(nz, cx, cy)
    store.wait()


def keep(listing, rows, valid):
    index = lax.broadcasted_iota(i32, listing.shape, 0)
    return jnp.where((index < rows) & jnp.logical_not(valid), 0.0, listing)


def relay_first_kernel(buffer, got, listing, merged, message, *, capacity, head):
    g = lax.axis_index("gx")
    species = buffer.shape[0]
    count = listing.shape[0]
    value = take_in(buffer[...], get_pieces(got, head + count, species), g % 2 == 1, capacity)
    merged[...] = value
    message[:count, :] = listing[...]
    put_pieces(message, count, first_send(value, (g // 2) % 2 == 1, 2 * capacity))


def near_kernel(base, listing, near_e, near_o, field, lists, left, right, *, grid_count):
    nz, cx, cy = base.shape[0], base.shape[1] // 2, base.shape[2]
    m, head = nz * cx, nz // 2 * cx
    count = listing.shape[0]
    rows = count // 3
    g = lax.axis_index("gx")
    even = g % 2 == 0
    e, o = near_e[head : head + count, :].astype(f32), near_o[head : head + count, :].astype(f32)
    lists[0] = keep(jnp.where(even, e, o), rows, g + 1 < grid_count)
    lists[1] = keep(jnp.where(even, o, e), rows, g >= 1)
    one_hots(lists, 0, -m // 2, m, -2 * cy, 2 * cy, left, right, 0)
    one_hots(lists, 1, -m // 2, m, 0, 2 * cy, left, right, 1)
    total = product(left[...], right[...])
    field[:, :cx, :] = base[:, :cx, :] - total[:, :cy].reshape(nz, cx, cy)
    field[:, cx:, :] = base[:, cx:, :] - total[:, cy:].reshape(nz, cx, cy)


def far_kernel(
    base, buffer, near_e, near_o, far_e, far_o, field, strips, strip_even, strip_odd, merged, send,
    lists, left, right, *, grid_count, capacity, after,
):
    nz, cx, cy = base.shape[0], base.shape[1] // 2, base.shape[2]
    half, zh = cx // 2, nz // 2
    head, m = zh * cx, nz * cx
    count = far_o.shape[0]
    rows = count // 3
    agents = rows * LANES
    g = lax.axis_index("gx")
    even = g % 2 == 0
    low_pair = g % 4 < 2
    fe, fo = far_e[:count, :].astype(f32), far_o[...].astype(f32)
    for which, listing, valid in (
        (0, jnp.where(low_pair, fe, fo), g + 2 < grid_count),
        (1, jnp.where(low_pair, fo, fe), g >= 2),
    ):
        code = listing[rows : 2 * rows].astype(i32) + m // 2
        at_z = code // cx
        code = (at_z % zh) * cx + (at_z // zh) * half + code % half
        lists[which, :rows] = jnp.where(valid, listing[:rows], 0.0)
        lists[which, rows : 2 * rows] = code.astype(f32)
        lists[which, 2 * rows :] = listing[2 * rows :]
    one_hots(lists, 0, 0, head, -2 * cy, cy, left, right, 0)
    one_hots(lists, 1, 0, head, cy, cy, left, right, 1)
    past_after = product(left[:, :agents], right[:, :agents])
    past_before = product(left[:, agents:], right[:, agents:])

    e, o = near_e[:head, :].astype(f32), near_o[:head, :].astype(f32)
    shape = (zh, cx, cy)
    from_before = (jnp.where(g >= 1, jnp.where(even, o, e) + 1.0, 0.0) - past_before).reshape(shape)
    from_after = (jnp.where(g + 1 < grid_count, jnp.where(even, e, o) + 1.0, 0.0) - past_after).reshape(shape)
    low = lax.broadcasted_iota(i32, shape, 1) < half
    field[:zh, :cx] = base[:zh, :cx] + jnp.where(low, from_before, 0.0)
    field[zh:, :cx] = base[zh:, :cx] + jnp.where(low, pltpu.roll(from_before, half, 1), 0.0)
    field[:zh, cx:] = base[:zh, cx:] + jnp.where(low, 0.0, pltpu.roll(from_after, half, 1))
    field[zh:, cx:] = base[zh:, cx:] + jnp.where(low, 0.0, from_after)

    edge = 2 * sweeps
    picked = lax.broadcasted_iota(i32, (2 * edge, cy), 0)
    picked = jnp.where(picked < edge, picked, picked + cy - 2 * edge)
    picker = (picked == lax.broadcasted_iota(i32, (2 * edge, cy), 1)).astype(f32).astype(bf16)
    flat = field[...].reshape(2 * m, cy)
    rims = sum(product(picker, piece) for piece in pieces(flat))
    strips[...] = rims
    h_even = lax.axis_index("gy") % 2 == 0
    head_rows, tail_rows = rims[:sweeps], rims[2 * edge - sweeps :]
    strip_even[...] = jnp.where(h_even, tail_rows, head_rows)
    strip_odd[...] = jnp.where(h_even, head_rows, tail_rows)
    value = take_in(buffer[...], get_pieces(far_e, count, buffer.shape[0]), (g // 2) % 2 == 1, 2 * capacity)
    merged[...] = value
    send[...] = first_send(value, (g // after) % 2 == 1, after * capacity)


def sweep_kernel(field, out, *, grid_count):
    nz, width, cy = field.shape
    half = width // 4
    g = lax.axis_index("gx")
    at_x = lax.broadcasted_iota(i32, (nz, width, cy), 1)
    outside = (g == 0) & (at_x < half) | (g == grid_count - 1) & (at_x >= width - half)
    scale = jnp.where(outside, 0.0, diffusion_number)
    centre = 1.0 / diffusion_number - 6.0
    plane = jnp.zeros((1, width, cy), f32)
    value = field[...]
    for turn in range(sweeps):
        total = jnp.concatenate([plane, value[:-1]], axis=0) + jnp.concatenate([value[1:], plane], axis=0)
        total = total + (pltpu.roll(value, 1, 1) + pltpu.roll(value, width - 1, 1))
        total = total + (pltpu.roll(value, 1, 2) + pltpu.roll(value, cy - 1, 2))
        value = (total + centre * value) * scale
    low = lax.broadcasted_iota(i32, (nz, width // 2, cy), 1) < half
    out[...] = pltpu.roll(jnp.where(low, value[:, width // 2 :], value[:, : width // 2]), half, 1)


def strip_kernel(
    inside, strips, got_even, got_odd, buffer, got, out, daughters, *, grid_count, row_count, capacity, step,
):
    daughters[...] = take_in(
        buffer[...], got[...], (lax.axis_index("gx") // step) % 2 == 1, capacity * step
    )
    nz, cx, cy = inside.shape
    m = strips.shape[1]
    width = m // nz
    g, h = lax.axis_index("gx"), lax.axis_index("gy")
    h_even = h % 2 == 0
    edge = 2 * sweeps
    has_right, has_left = h + 1 < row_count, h >= 1
    a, b = got_even[...], got_odd[...]
    right = jnp.where(has_right, jnp.where(h_even, a, b), 0.0)
    left = jnp.where(has_left, jnp.where(h_even, b, a), 0.0)
    band = jnp.concatenate([left, strips[...], right], axis=0)
    count = band.shape[0]
    lane = lax.broadcasted_iota(i32, (count, m), 1)
    line = lax.broadcasted_iota(i32, (count, m), 0)
    outside = (line < sweeps) & jnp.logical_not(has_left) | (line >= count - sweeps) & jnp.logical_not(has_right)
    at_x = lane % width
    outside = outside | (g == 0) & (at_x < cx // 2) | (g == grid_count - 1) & (at_x >= width - cx // 2)
    keep = jnp.where(outside, 0.0, diffusion_number)
    z_first, z_last = lane < width, lane >= m - width
    centre = 1.0 / diffusion_number - 6.0
    for turn in range(sweeps):
        total = jnp.where(z_first, 0.0, pltpu.roll(band, width, 1)) + jnp.where(z_last, 0.0, pltpu.roll(band, m - width, 1))
        total = total + (pltpu.roll(band, 1, 0) + pltpu.roll(band, count - 1, 0))
        total = total + (pltpu.roll(band, 1, 1) + pltpu.roll(band, m - 1, 1))
        band = (total + centre * band) * keep
    final = jnp.concatenate([band[sweeps : 2 * sweeps], band[count - 2 * sweeps : count - sweeps]], axis=0)
    placed = lax.broadcasted_iota(i32, (edge, cy), 0)
    placed = jnp.where(placed < sweeps, placed, placed + cy - edge)
    placer = (placed == lax.broadcasted_iota(i32, (edge, cy), 1)).astype(f32)
    edges = lax.dot_general(
        final, placer, (((0,), (0,)), ((), ())), precision=EXACT, preferred_element_type=f32
    ).reshape(nz, width, cy)
    low = lax.broadcasted_iota(i32, (nz, cx, cy), 1) < cx // 2
    mixed = pltpu.roll(jnp.where(low, edges[:, cx:], edges[:, :cx]), cx // 2, 1)
    at_y = lax.broadcasted_iota(i32, (nz, cx, cy), 2)
    out[...] = jnp.where((at_y < sweeps) | (at_y >= cy - sweeps), mixed, inside[...])


def pieces(value):
    high = value.astype(bf16)
    rest = value - high.astype(f32)
    middle = rest.astype(bf16)
    return high, middle, (rest - middle.astype(f32)).astype(bf16)


PIECE_ROWS = 48


def put_pieces(message, at, value):
    for number, piece in enumerate(pieces(value)):
        start = at + number * PIECE_ROWS
        message[start : start + value.shape[0], :] = piece


def get_pieces(message, at, count):
    starts = [at + number * PIECE_ROWS for number in range(3)]
    return sum(message[start : start + count, :].astype(f32) for start in starts)


def first_send(buffer, mine, width):
    count = buffer.shape[1]
    half = count // 2
    left, right = buffer[:, :half], buffer[:, half:]
    if width == half:
        return jnp.where(mine, left, right)
    bit = (lax.broadcasted_iota(i32, left.shape, 1) // width) % 2 == 1
    moved = jnp.where(mine, pltpu.roll(right, width, 1), pltpu.roll(right, half - width, 1))
    return jnp.where(jnp.logical_xor(bit, mine), left, moved)


def take_in(buffer, got, mine, width):
    count = buffer.shape[1]
    half = count // 2
    left, right = buffer[:, :half], buffer[:, half:]
    if width == half:
        left, right = jnp.where(mine, got, left), jnp.where(mine, right, got)
    else:
        bit = (lax.broadcasted_iota(i32, left.shape, 1) // width) % 2 == 1
        other = jnp.logical_xor(bit, mine)
        moved = jnp.where(mine, pltpu.roll(got, half - width, 1), pltpu.roll(got, width, 1))
        left, right = jnp.where(other, moved, left), jnp.where(other, got, right)
    return jnp.concatenate([left, right], axis=1)


def place_daughters(state, ids, target, capacity, columns):
    species, agents = state.shape
    picks = ids.shape[1]
    square = (picks, picks)
    across = jnp.broadcast_to(target, square)
    down = jnp.broadcast_to(column(target, picks), square)
    earlier = lax.broadcasted_iota(i32, square, 0) < lax.broadcasted_iota(i32, square, 1)
    rank = jnp.sum(jnp.where((across == down) & earlier, 1, 0), axis=0, keepdims=True)
    position = target * capacity + rank
    chosen = (lax.broadcasted_iota(i32, (agents, picks), 0) == ids).astype(f32).astype(bf16)
    mothers = sum(jnp.dot(p, chosen, preferred_element_type=f32) for p in pieces(state))
    placing = (lax.broadcasted_iota(i32, (columns, picks), 0) == position).astype(f32).astype(bf16)
    return sum(product(p, placing) for p in pieces(mothers))


def relay_kernel(buffer, got, merged, send, *, capacity, step, after):
    g = lax.axis_index("gx")
    value = take_in(buffer[...], got[...], (g // step) % 2 == 1, capacity * step)
    merged[...] = value
    send[...] = first_send(value, (g // after) % 2 == 1, capacity * after)


def solution(mesh):
    grid_count, row_count = mesh.shape["gx"], mesh.shape["gy"]

    def swap(value, partner):
        return lax.ppermute(value, GRID, swap_pairs(grid_count, row_count, partner))

    def side_odd(g, h):
        p = h + 1 if h % 2 else h - 1
        return (g, p) if 0 <= p < row_count else (g, h ^ (row_count - 1))

    def shards(
        cell_state, coupling, basal_rate, half_sat, decay_rate, uptake_weight,
        agent_counts, divider_ids, destinations, voxel_index, oxygen,
    ):
        species, agents = cell_state.shape
        nz, cx, cy = oxygen.shape
        picks = divider_ids.shape[0]
        rows = agents // LANES
        head = nz // 2 * cx
        capacity = max(2, 2 * picks // grid_count)
        columns = grid_count * capacity

        def line(value):
            return value.reshape(1, -1)

        def kernel(body, **sizes):
            def run(*refs):
                return body(*refs, **sizes)

            return run

        m = nz * cx
        count = 3 * rows
        pieces_rows = 3 * PIECE_ROWS
        one_field = (nz, 2 * cx, cy)
        listed = (count, LANES)
        half_buffer = ((species, columns // 2), f32)
        assert species <= PIECE_ROWS and columns == 2 * LANES and grid_count >= 8

        state, message_even, message_odd, listing, buffer = call(
            kernel(advance_kernel, cy=cy, cx=cx, nz=nz, capacity=capacity),
            [((species, agents), f32), ((head + count + pieces_rows, LANES), bf16), ((head + count, LANES), bf16),
             (listed, bf16), ((species, columns), f32)],
            "advance",
            [agent_counts, cell_state, coupling, line(basal_rate), line(half_sat), line(decay_rate),
             line(uptake_weight), voxel_index.reshape(rows, LANES), oxygen, line(divider_ids), line(destinations)],
            smem=(0,),
            hbm=range(1, 11),
            scratch=[pltpu.VMEM((species, agents), f32), pltpu.VMEM((species, species), f32)]
            + [pltpu.VMEM((1, species), f32)] * 4
            + [pltpu.VMEM((rows, LANES), i32), pltpu.VMEM((nz, cx, cy), f32)]
            + [pltpu.VMEM((1, picks), i32)] * 2
            + [pltpu.VMEM((rows, LANES), f32), pltpu.SemaphoreType.DMA((10,))],
        )
        near_e = swap(message_even, near_even)
        near_o = swap(message_odd, near_odd)
        base, new_state = call(
            own_kernel,
            [(one_field, f32), ((species, agents), f32)],
            "own",
            [oxygen, listing, state],
            hbm=(0, 4),
            scratch=[pltpu.VMEM((1,) + listed, f32), pltpu.VMEM((m, agents), bf16), pltpu.VMEM((2 * cy, agents), bf16),
                     pltpu.VMEM((nz, cx, cy), f32), pltpu.SemaphoreType.DMA((2,))],
        )
        buffer, base = lax.optimization_barrier((buffer, base))
        buffer, message_far = call(
            kernel(relay_first_kernel, capacity=capacity, head=head),
            [((species, columns), f32), ((count + pieces_rows, LANES), bf16)],
            "relay",
            [buffer, near_e, listing],
        )
        far_e = swap(message_far, far_even)
        far_o = swap(listing, far_odd)
        base, _ = lax.optimization_barrier((base, message_far))
        (field,) = call(
            kernel(near_kernel, grid_count=grid_count),
            [(one_field, f32)],
            "near",
            [base, listing, near_e, near_o],
            scratch=[pltpu.VMEM((2,) + listed, f32), pltpu.VMEM((m, 2 * agents), bf16),
                     pltpu.VMEM((2 * cy, 2 * agents), bf16)],
        )
        step = 4
        field, strips, strip_even, strip_odd, buffer, send = call(
            kernel(far_kernel, grid_count=grid_count, capacity=capacity, after=step),
            [(one_field, f32), ((4 * sweeps, 2 * m), f32), ((sweeps, 2 * m), f32), ((sweeps, 2 * m), f32),
             ((species, columns), f32)] + [half_buffer],
            "far",
            [field, buffer, near_e, near_o, far_e, far_o],
            scratch=[pltpu.VMEM((2,) + listed, f32), pltpu.VMEM((head, 2 * agents), bf16),
                     pltpu.VMEM((cy, 2 * agents), bf16)],
        )
        got_even = swap(strip_even, side_even)
        got_odd = swap(strip_odd, side_odd)
        got = swap(send, lambda g, h: (g ^ step, h))
        (inside,) = call(
            kernel(sweep_kernel, grid_count=grid_count), [((nz, cx, cy), f32)], "sweeps", [field]
        )
        while step < grid_count // 2:
            after = 2 * step
            buffer, sent = call(
                kernel(relay_kernel, capacity=capacity, step=step, after=after),
                [((species, columns), f32), half_buffer],
                "relay",
                [buffer, got],
            )
            step = after
            got = swap(sent, lambda g, h: (g ^ step, h))
        new_oxygen, daughter_state = call(
            kernel(strip_kernel, grid_count=grid_count, row_count=row_count, capacity=capacity, step=step),
            [((nz, cx, cy), f32), ((species, columns), f32)],
            "strips",
            [inside, strips, got_even, got_odd, buffer, got],
        )
        return new_state, daughter_state, new_oxygen

    return jax.shard_map(
        shards,
        mesh=mesh,
        in_specs=(
            P(None, GRID), P(), P(), P(), P(), P(), P(GRID), P(GRID), P(GRID, None), P(GRID), P(None, "gx", "gy"),
        ),
        out_specs=(P(None, GRID), P(None, GRID), P(None, "gx", "gy")),
        check_vma=False,
    )
```

```python
import jax
import jax.numpy as jnp
from jax import lax
from jax.experimental import pallas as pl
from jax.experimental.pallas import tpu as pltpu
from jax.sharding import PartitionSpec as P

time_step = 0.25
diffusion_number = 0.16
sweeps = 4
GRID = ("gx", "gy")
LANES = 128
AGENT_PART = 2048
EXACT = lax.Precision.HIGHEST
f32, bf16, i32 = jnp.float32, jnp.bfloat16, jnp.int32
VMEM_LIMIT = 48 << 20


def call(body, outs, name, inputs, smem=(), hbm=(), scratch=(), cost=None):
    def spec(at, shape):
        if at in smem:
            return pl.BlockSpec(memory_space=pltpu.SMEM)
        return pl.BlockSpec(memory_space=pltpu.HBM) if at in hbm else pl.BlockSpec(memory_space=pltpu.VMEM)

    count = len(inputs)
    inputs = [pltpu.with_memory_space_constraint(v, pltpu.HBM) if at in hbm else v for at, v in enumerate(inputs)]
    return pl.pallas_call(
        body,
        out_shape=tuple(jax.ShapeDtypeStruct(s, t) for s, t in outs),
        in_specs=[spec(at, value.shape) for at, value in enumerate(inputs)],
        out_specs=tuple(spec(count + at, s) for at, (s, t) in enumerate(outs)),
        scratch_shapes=scratch,
        compiler_params=pltpu.CompilerParams(vmem_limit_bytes=VMEM_LIMIT),
        name=name,
    )(*inputs)


def swap_pairs(grid_count, row_count, partner):
    pairs = []
    for g in range(grid_count):
        for h in range(row_count):
            p, q = partner(g, h)
            if not (0 <= p < grid_count and 0 <= q < row_count):
                p, q = g, h ^ 1
            pairs.append((g * row_count + h, p * row_count + q))
    return pairs


def near_even(g, h):
    return g ^ 1, h


def near_odd(g, h):
    return (g + 1 if g % 2 else g - 1), h


def far_even(g, h):
    return g ^ 2, h


def far_odd(g, h):
    return (g + 2 if g & 2 else g - 2), h


def side_even(g, h):
    return g, h ^ 1


def column(row, count):
    shape = (count, count)
    same = lax.broadcasted_iota(i32, shape, 0) == lax.broadcasted_iota(i32, shape, 1)
    return jnp.sum(jnp.where(same, jnp.broadcast_to(row, shape), 0), axis=1, keepdims=True)


def advance_kernel(
    count_ref, cell_hbm, coupling_hbm, basal_hbm, half_hbm, decay_hbm, weight_hbm, voxel_hbm, oxygen_hbm, ids_hbm,
    targets_hbm, new_state, message_even, message_odd, message_far, buffer,
    cell, coupling, basal, half, decay, weight, voxel, oxygen, ids, targets, drive, matrices, stack, semaphores,
    *, cy, cx, nz, capacity,
):
    pairs = (
        (coupling_hbm, coupling), (basal_hbm, basal), (half_hbm, half), (decay_hbm, decay), (weight_hbm, weight),
        (voxel_hbm, voxel), (ids_hbm, ids), (targets_hbm, targets), (oxygen_hbm, oxygen),
    )
    species, agents = cell.shape
    parts = [slice(at, at + AGENT_PART) for at in range(0, agents, AGENT_PART)]
    copies = [pltpu.make_async_copy(a, b, semaphores.at[i]) for i, (a, b) in enumerate(pairs)]
    waves = [
        pltpu.make_async_copy(cell_hbm.at[:, part], cell.at[:, part], semaphores.at[len(pairs) + i])
        for i, part in enumerate(parts)
    ]
    waves[0].start()
    stack[...] = jnp.zeros_like(stack)
    for copy in copies[:-1]:
        copy.start()
    for copy in waves[1:] + copies[-1:]:
        copy.start()
    for copy in copies[:-1]:
        copy.wait()
    basal_c, half_c, decay_c, weight_c = (column(r[...], species) for r in (basal, half, decay, weight))
    half_square = half_c * half_c
    matrix_high, matrix_low, _ = pieces(coupling[...])
    matrices[...] = jnp.zeros_like(matrices)
    for number, piece in enumerate((matrix_high, matrix_high, matrix_low)):
        matrices[:, number * PIECE_ROWS : number * PIECE_ROWS + species] = piece
    matrix = matrices[...]

    def rates(current):
        square = current * current
        occupancy = square / (half_square + square)
        high = occupancy.astype(bf16)
        low = (occupancy - high.astype(f32)).astype(bf16)
        for number, piece in enumerate((high, low, high)):
            stack[number * PIECE_ROWS : number * PIECE_ROWS + species, :] = piece
        drive_sum = jnp.dot(matrix, stack[...], preferred_element_type=f32)
        return basal_c + drive_sum - decay_c * current

    rows = agents // LANES
    picks = ids.shape[1]
    mothers = jnp.zeros((species, picks), f32)
    for part, wave in zip(parts, waves):
        wave.wait()
        current = cell[:, part]
        for substep in range(2):
            middle = current + (0.5 * time_step) * rates(current)
            current = current + time_step * rates(middle)
        new_state[:, part] = current
        total = jnp.sum(weight_c * current, axis=0, keepdims=True)
        for at in range(0, AGENT_PART, LANES):
            c = (part.start + at) // LANES
            drive[c : c + 1, :] = total[:, at : at + LANES]
        slots = lax.broadcasted_iota(i32, (AGENT_PART, picks), 0) + part.start
        chosen = (slots == ids[...]).astype(f32).astype(bf16)
        mothers += sum(jnp.dot(p, chosen, preferred_element_type=f32) for p in pieces(current)[:2])
    copies[-1].wait()
    x = drive[...]
    soft = jnp.maximum(x, 0.0) + jnp.log1p(jnp.exp(-jnp.abs(x)))
    slot = lax.broadcasted_iota(i32, (rows, LANES), 0) * LANES + lax.broadcasted_iota(i32, (rows, LANES), 1)
    uptake = jnp.where(slot < count_ref[0], soft, 0.0)
    code = voxel[...]
    at_y = code % cy
    at_x = (code // cy) % cx
    at_z = (code // (cy * cx)) % nz
    slab_x = (code // (cy * cx * nz)) * cx + at_x + cx // 2
    row = at_z * cx + slab_x % cx - nz * cx // 2
    col = (slab_x // cx) * cy + at_y - 2 * cy
    listing = jnp.concatenate([uptake, row.astype(f32), col.astype(f32)], axis=0).astype(bf16)
    own = oxygen[...] - 1.0
    turned = pltpu.roll(own, cx // 2, 1)
    low = lax.broadcasted_iota(i32, (nz // 2, cx, cy), 1) < cx // 2
    a, b = own[: nz // 2], own[nz // 2 :]
    ta, tb = turned[: nz // 2], turned[nz // 2 :]
    upper = jnp.where(low, ta, b)
    lower = jnp.where(low, a, tb)
    even = lax.axis_index("gx") % 2 == 0
    to_next = upper.reshape(nz // 2 * cx, cy)
    to_previous = lower.reshape(nz // 2 * cx, cy)
    head = nz // 2 * cx
    message_even[:head, :] = jnp.where(even, to_next, to_previous).astype(bf16)
    message_odd[:head, :] = jnp.where(even, to_previous, to_next).astype(bf16)
    tail = head + 3 * rows
    message_even[head:tail, :] = listing
    message_odd[head:, :] = listing
    message_far[...] = listing
    placed = place_daughters(mothers, targets[...], capacity, buffer.shape[1])
    buffer[...] = placed
    put_pieces(message_even, tail, first_send(placed, lax.axis_index("gx") % 2 == 1, capacity))


def one_hots(lists, which, first, m, base, width, left, right, slot):
    rows = lists.shape[1] // 3
    pack = 16
    row_at = (lax.broadcasted_iota(i32, (m, LANES), 0) + first).astype(f32).astype(bf16).reshape(m // pack, pack, LANES)
    col_at = (lax.broadcasted_iota(i32, (width, LANES), 0) + base).astype(f32).astype(bf16)
    col_at = col_at.reshape(width // pack, pack, LANES)
    one, zero = jnp.ones((), bf16), jnp.zeros((), bf16)

    def line(at):
        return jnp.broadcast_to(lists[which, at : at + 1, :], (pack, LANES)).astype(bf16)[None]

    for at in range(rows):
        columns = slice((slot * rows + at) * LANES, (slot * rows + at + 1) * LANES)
        hit = jnp.where(row_at == line(rows + at), one, zero)
        left[:, columns] = hit.reshape(m, LANES)
        spread = jnp.where(col_at == line(2 * rows + at), jnp.broadcast_to(line(at), col_at.shape), zero)
        right[:width, columns] = spread.reshape(width, LANES)


def product(left, right):
    return lax.dot_general(left, right, (((1,), (1,)), ((), ())), preferred_element_type=f32)


def own_kernel(oxygen_hbm, own_list, state, base, new_state, lists, left, right, oxygen, semaphores):
    copy = pltpu.make_async_copy(oxygen_hbm, oxygen, semaphores.at[0])
    copy.start()
    store = pltpu.make_async_copy(state, new_state, semaphores.at[1])
    store.start()
    nz, cx, cy = oxygen.shape
    m = nz * cx
    lists[0] = own_list[...].astype(f32)
    one_hots(lists, 0, -m // 2, m, -cy, 2 * cy, left, right, 0)
    total = product(left[...], right[...])
    copy.wait()
    low = lax.broadcasted_iota(i32, (nz, cx, cy), 1) < cx // 2
    inner = pltpu.roll(oxygen[...], cx // 2, 1)
    base[:, :cx, :] = jnp.where(low, 0.0, inner) - total[:, :cy].reshape(nz, cx, cy)
    base[:, cx:, :] = jnp.where(low, inner, 0.0) - total[:, cy:].reshape(nz, cx, cy)
    store.wait()


def keep(listing, rows, valid):
    index = lax.broadcasted_iota(i32, listing.shape, 0)
    return jnp.where((index < rows) & jnp.logical_not(valid), 0.0, listing)


def relay_first_kernel(buffer, got, listing, merged, message, *, capacity, head):
    g = lax.axis_index("gx")
    species = buffer.shape[0]
    count = listing.shape[0]
    value = take_in(buffer[...], get_pieces(got, head + count, species), g % 2 == 1, capacity)
    merged[...] = value
    message[:count, :] = listing[...]
    put_pieces(message, count, first_send(value, (g // 2) % 2 == 1, 2 * capacity))


def near_kernel(base, listing, near_e, near_o, field, lists, left, right, *, grid_count):
    nz, cx, cy = base.shape[0], base.shape[1] // 2, base.shape[2]
    m, head = nz * cx, nz // 2 * cx
    count = listing.shape[0]
    rows = count // 3
    g = lax.axis_index("gx")
    even = g % 2 == 0
    e, o = near_e[head : head + count, :].astype(f32), near_o[head : head + count, :].astype(f32)
    lists[0] = keep(jnp.where(even, e, o), rows, g + 1 < grid_count)
    lists[1] = keep(jnp.where(even, o, e), rows, g >= 1)
    one_hots(lists, 0, -m // 2, m, -2 * cy, 2 * cy, left, right, 0)
    one_hots(lists, 1, -m // 2, m, 0, 2 * cy, left, right, 1)
    total = product(left[...], right[...])
    field[:, :cx, :] = base[:, :cx, :] - total[:, :cy].reshape(nz, cx, cy)
    field[:, cx:, :] = base[:, cx:, :] - total[:, cy:].reshape(nz, cx, cy)


def far_kernel(
    base, buffer, near_e, near_o, far_e, far_o, field, strips, strip_even, strip_odd, merged, send,
    lists, left, right, *, grid_count, capacity, after,
):
    nz, cx, cy = base.shape[0], base.shape[1] // 2, base.shape[2]
    half, zh = cx // 2, nz // 2
    head, m = zh * cx, nz * cx
    count = far_o.shape[0]
    rows = count // 3
    agents = rows * LANES
    g = lax.axis_index("gx")
    even = g % 2 == 0
    low_pair = g % 4 < 2
    fe, fo = far_e[:count, :].astype(f32), far_o[...].astype(f32)
    for which, listing, valid in (
        (0, jnp.where(low_pair, fe, fo), g + 2 < grid_count),
        (1, jnp.where(low_pair, fo, fe), g >= 2),
    ):
        code = listing[rows : 2 * rows].astype(i32) + m // 2
        at_z = code // cx
        code = (at_z % zh) * cx + (at_z // zh) * half + code % half
        lists[which, :rows] = jnp.where(valid, listing[:rows], 0.0)
        lists[which, rows : 2 * rows] = code.astype(f32)
        lists[which, 2 * rows :] = listing[2 * rows :]
    one_hots(lists, 0, 0, head, -2 * cy, cy, left, right, 0)
    one_hots(lists, 1, 0, head, cy, cy, left, right, 1)
    past_after = product(left[:, :agents], right[:, :agents])
    past_before = product(left[:, agents:], right[:, agents:])

    e, o = near_e[:head, :].astype(f32), near_o[:head, :].astype(f32)
    shape = (zh, cx, cy)
    from_before = (jnp.where(g >= 1, jnp.where(even, o, e) + 1.0, 0.0) - past_before).reshape(shape)
    from_after = (jnp.where(g + 1 < grid_count, jnp.where(even, e, o) + 1.0, 0.0) - past_after).reshape(shape)
    low = lax.broadcasted_iota(i32, shape, 1) < half
    field[:zh, :cx] = base[:zh, :cx] + jnp.where(low, from_before, 0.0)
    field[zh:, :cx] = base[zh:, :cx] + jnp.where(low, pltpu.roll(from_before, half, 1), 0.0)
    field[:zh, cx:] = base[:zh, cx:] + jnp.where(low, 0.0, pltpu.roll(from_after, half, 1))
    field[zh:, cx:] = base[zh:, cx:] + jnp.where(low, 0.0, from_after)

    edge = 2 * sweeps
    picked = lax.broadcasted_iota(i32, (2 * edge, cy), 0)
    picked = jnp.where(picked < edge, picked, picked + cy - 2 * edge)
    picker = (picked == lax.broadcasted_iota(i32, (2 * edge, cy), 1)).astype(f32).astype(bf16)
    flat = field[...].reshape(2 * m, cy)
    rims = sum(product(picker, piece) for piece in pieces(flat)[:2])
    strips[...] = rims
    h_even = lax.axis_index("gy") % 2 == 0
    head_rows, tail_rows = rims[:sweeps], rims[2 * edge - sweeps :]
    strip_even[...] = jnp.where(h_even, tail_rows, head_rows)
    strip_odd[...] = jnp.where(h_even, head_rows, tail_rows)
    value = take_in(buffer[...], get_pieces(far_e, count, buffer.shape[0]), (g // 2) % 2 == 1, 2 * capacity)
    merged[...] = value
    send[...] = first_send(value, (g // after) % 2 == 1, after * capacity)


def sweep_kernel(field, out, *, grid_count):
    nz, width, cy = field.shape
    half = width // 4
    g = lax.axis_index("gx")
    at_x = lax.broadcasted_iota(i32, (nz, width, cy), 1)
    outside = (g == 0) & (at_x < half) | (g == grid_count - 1) & (at_x >= width - half)
    scale = jnp.where(outside, 0.0, diffusion_number)
    centre = 1.0 / diffusion_number - 6.0
    plane = jnp.zeros((1, width, cy), f32)
    value = field[...]
    for turn in range(sweeps):
        total = jnp.concatenate([plane, value[:-1]], axis=0) + jnp.concatenate([value[1:], plane], axis=0)
        total = total + (pltpu.roll(value, 1, 1) + pltpu.roll(value, width - 1, 1))
        total = total + (pltpu.roll(value, 1, 2) + pltpu.roll(value, cy - 1, 2))
        value = (total + centre * value) * scale
    low = lax.broadcasted_iota(i32, (nz, width // 2, cy), 1) < half
    out[...] = pltpu.roll(jnp.where(low, value[:, width // 2 :], value[:, : width // 2]), half, 1)


def strip_kernel(
    inside, strips, got_even, got_odd, buffer, got, out, daughters, *, grid_count, row_count, capacity, step,
):
    daughters[...] = take_in(
        buffer[...], got[...], (lax.axis_index("gx") // step) % 2 == 1, capacity * step
    )
    nz, cx, cy = inside.shape
    m = strips.shape[1]
    width = m // nz
    g, h = lax.axis_index("gx"), lax.axis_index("gy")
    h_even = h % 2 == 0
    edge = 2 * sweeps
    has_right, has_left = h + 1 < row_count, h >= 1
    a, b = got_even[...], got_odd[...]
    right = jnp.where(has_right, jnp.where(h_even, a, b), 0.0)
    left = jnp.where(has_left, jnp.where(h_even, b, a), 0.0)
    band = jnp.concatenate([left, strips[...], right], axis=0)
    count = band.shape[0]
    lane = lax.broadcasted_iota(i32, (count, m), 1)
    line = lax.broadcasted_iota(i32, (count, m), 0)
    outside = (line < sweeps) & jnp.logical_not(has_left) | (line >= count - sweeps) & jnp.logical_not(has_right)
    at_x = lane % width
    outside = outside | (g == 0) & (at_x < cx // 2) | (g == grid_count - 1) & (at_x >= width - cx // 2)
    keep = jnp.where(outside, 0.0, diffusion_number)
    z_first, z_last = lane < width, lane >= m - width
    centre = 1.0 / diffusion_number - 6.0
    for turn in range(sweeps):
        total = jnp.where(z_first, 0.0, pltpu.roll(band, width, 1)) + jnp.where(z_last, 0.0, pltpu.roll(band, m - width, 1))
        total = total + (pltpu.roll(band, 1, 0) + pltpu.roll(band, count - 1, 0))
        total = total + (pltpu.roll(band, 1, 1) + pltpu.roll(band, m - 1, 1))
        band = (total + centre * band) * keep
    final = jnp.concatenate([band[sweeps : 2 * sweeps], band[count - 2 * sweeps : count - sweeps]], axis=0)
    placed = lax.broadcasted_iota(i32, (edge, cy), 0)
    placed = jnp.where(placed < sweeps, placed, placed + cy - edge)
    placer = (placed == lax.broadcasted_iota(i32, (edge, cy), 1)).astype(f32)
    high = final.astype(bf16).astype(f32)
    stacked = jnp.concatenate([high, final - high], axis=0).astype(bf16)
    placers = jnp.concatenate([placer, placer], axis=0).astype(bf16)
    edges = lax.dot_general(
        stacked, placers, (((0,), (0,)), ((), ())), preferred_element_type=f32
    ).reshape(nz, width, cy)
    low = lax.broadcasted_iota(i32, (nz, cx, cy), 1) < cx // 2
    mixed = pltpu.roll(jnp.where(low, edges[:, cx:], edges[:, :cx]), cx // 2, 1)
    at_y = lax.broadcasted_iota(i32, (nz, cx, cy), 2)
    out[...] = jnp.where((at_y < sweeps) | (at_y >= cy - sweeps), mixed, inside[...])


def pieces(value):
    high = value.astype(bf16)
    rest = value - high.astype(f32)
    middle = rest.astype(bf16)
    return high, middle, (rest - middle.astype(f32)).astype(bf16)


PIECE_ROWS = 48


def put_pieces(message, at, value):
    for number, piece in enumerate(pieces(value)[:2]):
        start = at + number * PIECE_ROWS
        message[start : start + value.shape[0], :] = piece


def get_pieces(message, at, count):
    starts = [at + number * PIECE_ROWS for number in range(2)]
    return sum(message[start : start + count, :].astype(f32) for start in starts)


def first_send(buffer, mine, width):
    count = buffer.shape[1]
    half = count // 2
    left, right = buffer[:, :half], buffer[:, half:]
    if width == half:
        return jnp.where(mine, left, right)
    bit = (lax.broadcasted_iota(i32, left.shape, 1) // width) % 2 == 1
    moved = jnp.where(mine, pltpu.roll(right, width, 1), pltpu.roll(right, half - width, 1))
    return jnp.where(jnp.logical_xor(bit, mine), left, moved)


def take_in(buffer, got, mine, width):
    count = buffer.shape[1]
    half = count // 2
    left, right = buffer[:, :half], buffer[:, half:]
    if width == half:
        left, right = jnp.where(mine, got, left), jnp.where(mine, right, got)
    else:
        bit = (lax.broadcasted_iota(i32, left.shape, 1) // width) % 2 == 1
        other = jnp.logical_xor(bit, mine)
        moved = jnp.where(mine, pltpu.roll(got, half - width, 1), pltpu.roll(got, width, 1))
        left, right = jnp.where(other, moved, left), jnp.where(other, got, right)
    return jnp.concatenate([left, right], axis=1)


def place_daughters(mothers, target, capacity, columns):
    picks = target.shape[1]
    square = (picks, picks)
    across = jnp.broadcast_to(target, square)
    down = jnp.broadcast_to(column(target, picks), square)
    earlier = lax.broadcasted_iota(i32, square, 0) < lax.broadcasted_iota(i32, square, 1)
    rank = jnp.sum(jnp.where((across == down) & earlier, 1, 0), axis=0, keepdims=True)
    position = target * capacity + rank
    placing = (lax.broadcasted_iota(i32, (columns, picks), 0) == position).astype(f32).astype(bf16)
    return sum(product(p, placing) for p in pieces(mothers)[:2])


def relay_kernel(buffer, got, merged, send, *, capacity, step, after):
    g = lax.axis_index("gx")
    value = take_in(buffer[...], got[...], (g // step) % 2 == 1, capacity * step)
    merged[...] = value
    send[...] = first_send(value, (g // after) % 2 == 1, capacity * after)


def solution(mesh):
    grid_count, row_count = mesh.shape["gx"], mesh.shape["gy"]

    def swap(value, partner):
        return lax.ppermute(value, GRID, swap_pairs(grid_count, row_count, partner))

    def side_odd(g, h):
        p = h + 1 if h % 2 else h - 1
        return (g, p) if 0 <= p < row_count else (g, h ^ (row_count - 1))

    def shards(
        cell_state, coupling, basal_rate, half_sat, decay_rate, uptake_weight,
        agent_counts, divider_ids, destinations, voxel_index, oxygen,
    ):
        species, agents = cell_state.shape
        nz, cx, cy = oxygen.shape
        picks = divider_ids.shape[0]
        rows = agents // LANES
        head = nz // 2 * cx
        capacity = max(2, 2 * picks // grid_count)
        columns = grid_count * capacity

        def line(value):
            return value.reshape(1, -1)

        def kernel(body, **sizes):
            def run(*refs):
                return body(*refs, **sizes)

            return run

        m = nz * cx
        count = 3 * rows
        pieces_rows = 2 * PIECE_ROWS
        one_field = (nz, 2 * cx, cy)
        listed = (count, LANES)
        half_buffer = ((species, columns // 2), f32)
        assert species <= PIECE_ROWS and columns == 2 * LANES and grid_count >= 8

        state, message_even, message_odd, listing, buffer = call(
            kernel(advance_kernel, cy=cy, cx=cx, nz=nz, capacity=capacity),
            [((species, agents), f32), ((head + count + pieces_rows, LANES), bf16), ((head + count, LANES), bf16),
             (listed, bf16), ((species, columns), f32)],
            "advance",
            [agent_counts, cell_state, coupling, line(basal_rate), line(half_sat), line(decay_rate),
             line(uptake_weight), voxel_index.reshape(rows, LANES), oxygen, line(divider_ids), line(destinations)],
            smem=(0,),
            hbm=range(1, 11),
            scratch=[pltpu.VMEM((species, agents), f32), pltpu.VMEM((species, species), f32)]
            + [pltpu.VMEM((1, species), f32)] * 4
            + [pltpu.VMEM((rows, LANES), i32), pltpu.VMEM((nz, cx, cy), f32)]
            + [pltpu.VMEM((1, picks), i32)] * 2
            + [pltpu.VMEM((rows, LANES), f32), pltpu.VMEM((species, 3 * PIECE_ROWS), bf16),
               pltpu.VMEM((3 * PIECE_ROWS, AGENT_PART), bf16), pltpu.SemaphoreType.DMA((9 + agents // AGENT_PART,))],
        )
        near_e = swap(message_even, near_even)
        near_o = swap(message_odd, near_odd)
        base, new_state = call(
            own_kernel,
            [(one_field, f32), ((species, agents), f32)],
            "own",
            [oxygen, listing, state],
            hbm=(0, 4),
            scratch=[pltpu.VMEM((1,) + listed, f32), pltpu.VMEM((m, agents), bf16), pltpu.VMEM((2 * cy, agents), bf16),
                     pltpu.VMEM((nz, cx, cy), f32), pltpu.SemaphoreType.DMA((2,))],
        )
        buffer, base = lax.optimization_barrier((buffer, base))
        buffer, message_far = call(
            kernel(relay_first_kernel, capacity=capacity, head=head),
            [((species, columns), f32), ((count + pieces_rows, LANES), bf16)],
            "relay",
            [buffer, near_e, listing],
        )
        far_e = swap(message_far, far_even)
        far_o = swap(listing, far_odd)
        base, _ = lax.optimization_barrier((base, message_far))
        (field,) = call(
            kernel(near_kernel, grid_count=grid_count),
            [(one_field, f32)],
            "near",
            [base, listing, near_e, near_o],
            scratch=[pltpu.VMEM((2,) + listed, f32), pltpu.VMEM((m, 2 * agents), bf16),
                     pltpu.VMEM((2 * cy, 2 * agents), bf16)],
        )
        step = 4
        field, strips, strip_even, strip_odd, buffer, send = call(
            kernel(far_kernel, grid_count=grid_count, capacity=capacity, after=step),
            [(one_field, f32), ((4 * sweeps, 2 * m), f32), ((sweeps, 2 * m), f32), ((sweeps, 2 * m), f32),
             ((species, columns), f32)] + [half_buffer],
            "far",
            [field, buffer, near_e, near_o, far_e, far_o],
            scratch=[pltpu.VMEM((2,) + listed, f32), pltpu.VMEM((head, 2 * agents), bf16),
                     pltpu.VMEM((cy, 2 * agents), bf16)],
        )
        got = swap(send, lambda g, h: (g ^ step, h))
        got_odd = swap(strip_odd, side_odd)
        got_even = swap(strip_even, side_even)
        (inside,) = call(
            kernel(sweep_kernel, grid_count=grid_count), [((nz, cx, cy), f32)], "sweeps", [field]
        )
        while step < grid_count // 2:
            after = 2 * step
            buffer, sent = call(
                kernel(relay_kernel, capacity=capacity, step=step, after=after),
                [((species, columns), f32), half_buffer],
                "relay",
                [buffer, got],
            )
            step = after
            got = swap(sent, lambda g, h: (g ^ step, h))
        new_oxygen, daughter_state = call(
            kernel(strip_kernel, grid_count=grid_count, row_count=row_count, capacity=capacity, step=step),
            [((nz, cx, cy), f32), ((species, columns), f32)],
            "strips",
            [inside, strips, got_even, got_odd, buffer, got],
        )
        return new_state, daughter_state, new_oxygen

    return jax.shard_map(
        shards,
        mesh=mesh,
        in_specs=(
            P(None, GRID), P(), P(), P(), P(), P(), P(GRID), P(GRID), P(GRID, None), P(GRID), P(None, "gx", "gy"),
        ),
        out_specs=(P(None, GRID), P(None, GRID), P(None, "gx", "gy")),
        check_vma=False,
    )
```

```python
import jax
import jax.numpy as jnp
from jax import lax
from jax.experimental import pallas as pl
from jax.experimental.pallas import tpu as pltpu
from jax.sharding import PartitionSpec as P

time_step = 0.25
diffusion_number = 0.16
sweeps = 4
GRID = ("gx", "gy")
LANES = 128
EXACT = lax.Precision.HIGHEST
f32, bf16, i32 = jnp.float32, jnp.bfloat16, jnp.int32
VMEM_LIMIT = 48 << 20


def call(body, outs, name, inputs, smem=(), hbm=(), scratch=(), cost=None):
    def spec(at, shape):
        if at in smem:
            return pl.BlockSpec(memory_space=pltpu.SMEM)
        return pl.BlockSpec(memory_space=pltpu.HBM) if at in hbm else pl.BlockSpec(memory_space=pltpu.VMEM)

    count = len(inputs)
    inputs = [pltpu.with_memory_space_constraint(v, pltpu.HBM) if at in hbm else v for at, v in enumerate(inputs)]
    return pl.pallas_call(
        body,
        out_shape=tuple(jax.ShapeDtypeStruct(s, t) for s, t in outs),
        in_specs=[spec(at, value.shape) for at, value in enumerate(inputs)],
        out_specs=tuple(spec(count + at, s) for at, (s, t) in enumerate(outs)),
        scratch_shapes=scratch,
        compiler_params=pltpu.CompilerParams(vmem_limit_bytes=VMEM_LIMIT),
        name=name,
    )(*inputs)


def swap_pairs(grid_count, row_count, partner):
    pairs = []
    for g in range(grid_count):
        for h in range(row_count):
            p, q = partner(g, h)
            if not (0 <= p < grid_count and 0 <= q < row_count):
                p, q = g, h ^ 1
            pairs.append((g * row_count + h, p * row_count + q))
    return pairs


def near_even(g, h):
    return g ^ 1, h


def near_odd(g, h):
    return (g + 1 if g % 2 else g - 1), h


def far_even(g, h):
    return g ^ 2, h


def far_odd(g, h):
    return (g + 2 if g & 2 else g - 2), h


def side_even(g, h):
    return g, h ^ 1


def column(row, count):
    shape = (count, count)
    same = lax.broadcasted_iota(i32, shape, 0) == lax.broadcasted_iota(i32, shape, 1)
    return jnp.sum(jnp.where(same, jnp.broadcast_to(row, shape), 0), axis=1, keepdims=True)


def advance_kernel(
    count_ref, cell_hbm, coupling_hbm, basal_hbm, half_hbm, decay_hbm, weight_hbm, voxel_hbm, oxygen_hbm, ids_hbm,
    targets_hbm, new_state, message_even, message_odd, message_far, buffer,
    cell, coupling, basal, half, decay, weight, voxel, oxygen, ids, targets, drive, matrices, stack, chosen, codes, semaphores,
    *, cy, cx, nz, capacity,
):
    pairs = (
        (ids_hbm, ids), (voxel_hbm, voxel), (targets_hbm, targets), (coupling_hbm, coupling), (basal_hbm, basal),
        (half_hbm, half), (decay_hbm, decay), (weight_hbm, weight), (cell_hbm, cell), (oxygen_hbm, oxygen),
    )
    species, agents = cell.shape
    copies = [pltpu.make_async_copy(a, b, semaphores.at[i]) for i, (a, b) in enumerate(pairs)]
    for copy in copies:
        copy.start()
    stack[...] = jnp.zeros_like(stack)
    for copy in copies[:-2]:
        copy.wait()
    rows = agents // LANES
    picks = ids.shape[1]
    chosen[...] = (lax.broadcasted_iota(i32, (agents, picks), 0) == ids[...]).astype(f32).astype(bf16)
    code = voxel[...]
    at_y = code % cy
    at_x = (code // cy) % cx
    at_z = (code // (cy * cx)) % nz
    slab_x = (code // (cy * cx * nz)) * cx + at_x + cx // 2
    codes[:rows, :] = (at_z * cx + slab_x % cx - nz * cx // 2).astype(f32)
    codes[rows:, :] = ((slab_x // cx) * cy + at_y - 2 * cy).astype(f32)
    basal_c, half_c, decay_c, weight_c = (column(r[...], species) for r in (basal, half, decay, weight))
    half_square = half_c * half_c
    matrix_high, matrix_low, _ = pieces(coupling[...])
    matrices[...] = jnp.zeros_like(matrices)
    for number, piece in enumerate((matrix_high, matrix_high, matrix_low)):
        matrices[:, number * PIECE_ROWS : number * PIECE_ROWS + species] = piece
    matrix = matrices[...]

    def rates(current):
        square = current * current
        occupancy = square / (half_square + square)
        high = occupancy.astype(bf16)
        low = (occupancy - high.astype(f32)).astype(bf16)
        for number, piece in enumerate((high, low, high)):
            stack[number * PIECE_ROWS : number * PIECE_ROWS + species, :] = piece
        drive_sum = jnp.dot(matrix, stack[...], preferred_element_type=f32)
        return basal_c + drive_sum - decay_c * current

    placing = place_columns(targets[...], capacity, buffer.shape[1])
    copies[-2].wait()
    current = cell[...]
    for substep in range(2):
        middle = current + (0.5 * time_step) * rates(current)
        current = current + time_step * rates(middle)
    new_state[...] = current
    total = jnp.sum(weight_c * current, axis=0, keepdims=True)
    for c in range(rows):
        drive[c : c + 1, :] = total[:, c * LANES : (c + 1) * LANES]
    mothers = sum(jnp.dot(p, chosen[...], preferred_element_type=f32) for p in pieces(current)[:2])
    copies[-1].wait()
    x = drive[...]
    soft = jnp.maximum(x, 0.0) + jnp.log1p(jnp.exp(-jnp.abs(x)))
    slot = lax.broadcasted_iota(i32, (rows, LANES), 0) * LANES + lax.broadcasted_iota(i32, (rows, LANES), 1)
    uptake = jnp.where(slot < count_ref[0], soft, 0.0)
    listing = jnp.concatenate([uptake, codes[...]], axis=0).astype(bf16)
    own = oxygen[...] - 1.0
    turned = pltpu.roll(own, cx // 2, 1)
    low = lax.broadcasted_iota(i32, (nz // 2, cx, cy), 1) < cx // 2
    a, b = own[: nz // 2], own[nz // 2 :]
    ta, tb = turned[: nz // 2], turned[nz // 2 :]
    upper = jnp.where(low, ta, b)
    lower = jnp.where(low, a, tb)
    even = lax.axis_index("gx") % 2 == 0
    to_next = upper.reshape(nz // 2 * cx, cy)
    to_previous = lower.reshape(nz // 2 * cx, cy)
    head = nz // 2 * cx
    message_even[:head, :] = jnp.where(even, to_next, to_previous).astype(bf16)
    message_odd[:head, :] = jnp.where(even, to_previous, to_next).astype(bf16)
    tail = head + 3 * rows
    message_even[head:tail, :] = listing
    message_odd[head:, :] = listing
    message_far[...] = listing
    placed = sum(product(p, placing) for p in pieces(mothers)[:2])
    buffer[...] = placed
    put_pieces(message_even, tail, first_send(placed, lax.axis_index("gx") % 2 == 1, capacity))


def one_hots(lists, which, first, m, base, width, left, right, slot):
    rows = lists.shape[1] // 3
    pack = 16
    row_at = (lax.broadcasted_iota(i32, (m, LANES), 0) + first).astype(f32).astype(bf16).reshape(m // pack, pack, LANES)
    col_at = (lax.broadcasted_iota(i32, (width, LANES), 0) + base).astype(f32).astype(bf16)
    col_at = col_at.reshape(width // pack, pack, LANES)
    one, zero = jnp.ones((), bf16), jnp.zeros((), bf16)

    def line(at):
        return jnp.broadcast_to(lists[which, at : at + 1, :], (pack, LANES)).astype(bf16)[None]

    for at in range(rows):
        columns = slice((slot * rows + at) * LANES, (slot * rows + at + 1) * LANES)
        hit = jnp.where(row_at == line(rows + at), one, zero)
        left[:, columns] = hit.reshape(m, LANES)
        spread = jnp.where(col_at == line(2 * rows + at), jnp.broadcast_to(line(at), col_at.shape), zero)
        right[:width, columns] = spread.reshape(width, LANES)


def product(left, right):
    return lax.dot_general(left, right, (((1,), (1,)), ((), ())), preferred_element_type=f32)


def own_kernel(oxygen_hbm, own_list, state, base, new_state, lists, left, right, oxygen, semaphores):
    copy = pltpu.make_async_copy(oxygen_hbm, oxygen, semaphores.at[0])
    copy.start()
    store = pltpu.make_async_copy(state, new_state, semaphores.at[1])
    store.start()
    nz, cx, cy = oxygen.shape
    m = nz * cx
    lists[0] = own_list[...].astype(f32)
    one_hots(lists, 0, -m // 2, m, -cy, 2 * cy, left, right, 0)
    total = product(left[...], right[...])
    copy.wait()
    low = lax.broadcasted_iota(i32, (nz, cx, cy), 1) < cx // 2
    inner = pltpu.roll(oxygen[...], cx // 2, 1)
    base[:, :cx, :] = jnp.where(low, 0.0, inner) - total[:, :cy].reshape(nz, cx, cy)
    base[:, cx:, :] = jnp.where(low, inner, 0.0) - total[:, cy:].reshape(nz, cx, cy)
    store.wait()


def keep(listing, rows, valid):
    index = lax.broadcasted_iota(i32, listing.shape, 0)
    return jnp.where((index < rows) & jnp.logical_not(valid), 0.0, listing)


def relay_first_kernel(buffer, got, listing, merged, message, *, capacity, head):
    g = lax.axis_index("gx")
    species = buffer.shape[0]
    count = listing.shape[0]
    value = take_in(buffer[...], get_pieces(got, head + count, species), g % 2 == 1, capacity)
    merged[...] = value
    message[:count, :] = listing[...]
    put_pieces(message, count, first_send(value, (g // 2) % 2 == 1, 2 * capacity))


def near_kernel(base, listing, near_e, near_o, field, lists, left, right, *, grid_count):
    nz, cx, cy = base.shape[0], base.shape[1] // 2, base.shape[2]
    m, head = nz * cx, nz // 2 * cx
    count = listing.shape[0]
    rows = count // 3
    g = lax.axis_index("gx")
    even = g % 2 == 0
    e, o = near_e[head : head + count, :].astype(f32), near_o[head : head + count, :].astype(f32)
    lists[0] = keep(jnp.where(even, e, o), rows, g + 1 < grid_count)
    lists[1] = keep(jnp.where(even, o, e), rows, g >= 1)
    one_hots(lists, 0, -m // 2, m, -2 * cy, 2 * cy, left, right, 0)
    one_hots(lists, 1, -m // 2, m, 0, 2 * cy, left, right, 1)
    total = product(left[...], right[...])
    field[:, :cx, :] = base[:, :cx, :] - total[:, :cy].reshape(nz, cx, cy)
    field[:, cx:, :] = base[:, cx:, :] - total[:, cy:].reshape(nz, cx, cy)


def far_kernel(
    base, buffer, near_e, near_o, far_e, far_o, field, strips, strip_even, strip_odd, merged, send,
    lists, left, right, *, grid_count, capacity, after,
):
    nz, cx, cy = base.shape[0], base.shape[1] // 2, base.shape[2]
    half, zh = cx // 2, nz // 2
    head, m = zh * cx, nz * cx
    count = far_o.shape[0]
    rows = count // 3
    agents = rows * LANES
    g = lax.axis_index("gx")
    even = g % 2 == 0
    low_pair = g % 4 < 2
    fe, fo = far_e[:count, :].astype(f32), far_o[...].astype(f32)
    quarter = zh // 2
    for which, listing, base_code, valid in (
        (0, jnp.where(low_pair, fe, fo), -2 * cy, g + 2 < grid_count),
        (1, jnp.where(low_pair, fo, fe), cy, g >= 2),
    ):
        code = listing[rows : 2 * rows].astype(i32) + m // 2
        at_z, at_y = code // cx, listing[2 * rows :].astype(i32) - base_code
        inner_z = at_z % zh
        code = (inner_z % quarter) * cx + (inner_z // quarter) * half + code % half
        lists[which, :rows] = jnp.where(valid, listing[:rows], 0.0)
        lists[which, rows : 2 * rows] = code.astype(f32)
        lists[which, 2 * rows :] = jnp.where((at_y >= 0) & (at_y < cy), (at_z // zh) * cy + at_y, -1).astype(f32)
    one_hots(lists, 0, 0, head // 2, 0, 2 * cy, left, right, 0)
    one_hots(lists, 1, 0, head // 2, 0, 2 * cy, left, right, 1)
    low_quarter = lax.broadcasted_iota(i32, (quarter, cx, cy), 1) < half

    def unfold(total):
        lower, upper = (total[:, t * cy : (t + 1) * cy].reshape(quarter, cx, cy) for t in range(2))
        return jnp.concatenate(
            [
                jnp.where(low_quarter, lower, pltpu.roll(upper, half, 1)),
                jnp.where(low_quarter, pltpu.roll(lower, half, 1), upper),
            ],
            axis=0,
        )

    past_after = unfold(product(left[:, :agents], right[:, :agents]))
    past_before = unfold(product(left[:, agents:], right[:, agents:]))

    e, o = near_e[:head, :].astype(f32), near_o[:head, :].astype(f32)
    shape = (zh, cx, cy)
    from_before = jnp.where(g >= 1, jnp.where(even, o, e) + 1.0, 0.0).reshape(shape) - past_before
    from_after = jnp.where(g + 1 < grid_count, jnp.where(even, e, o) + 1.0, 0.0).reshape(shape) - past_after
    low = lax.broadcasted_iota(i32, shape, 1) < half
    field[:zh, :cx] = base[:zh, :cx] + jnp.where(low, from_before, 0.0)
    field[zh:, :cx] = base[zh:, :cx] + jnp.where(low, pltpu.roll(from_before, half, 1), 0.0)
    field[:zh, cx:] = base[:zh, cx:] + jnp.where(low, 0.0, pltpu.roll(from_after, half, 1))
    field[zh:, cx:] = base[zh:, cx:] + jnp.where(low, 0.0, from_after)

    edge = 2 * sweeps
    picked = lax.broadcasted_iota(i32, (2 * edge, cy), 0)
    picked = jnp.where(picked < edge, picked, picked + cy - 2 * edge)
    picker = (picked == lax.broadcasted_iota(i32, (2 * edge, cy), 1)).astype(f32).astype(bf16)
    tiles = 2 * m // LANES
    value = field[...].reshape(nz // tiles, tiles, 2 * cx, cy)
    flat = jnp.concatenate([value[:, k].reshape(LANES, cy) for k in range(tiles)], axis=0)
    rims = product(jnp.concatenate([picker, picker], axis=1), jnp.concatenate(pieces(flat)[:2], axis=1))
    strips[...] = rims
    h_even = lax.axis_index("gy") % 2 == 0
    head_rows, tail_rows = rims[:sweeps], rims[2 * edge - sweeps :]
    strip_even[...] = jnp.where(h_even, tail_rows, head_rows)
    strip_odd[...] = jnp.where(h_even, head_rows, tail_rows)
    value = take_in(buffer[...], get_pieces(far_e, count, buffer.shape[0]), (g // 2) % 2 == 1, 2 * capacity)
    merged[...] = value
    send[...] = first_send(value, (g // after) % 2 == 1, after * capacity)


def sweep_kernel(field, out, *, grid_count):
    nz, width, cy = field.shape
    half = width // 4
    g = lax.axis_index("gx")
    at_x = lax.broadcasted_iota(i32, (nz, width, cy), 1)
    outside = (g == 0) & (at_x < half) | (g == grid_count - 1) & (at_x >= width - half)
    scale = jnp.where(outside, 0.0, diffusion_number)
    centre = 1.0 / diffusion_number - 6.0
    plane = jnp.zeros((1, width, cy), f32)
    value = field[...]
    for turn in range(sweeps):
        total = jnp.concatenate([plane, value[:-1]], axis=0) + jnp.concatenate([value[1:], plane], axis=0)
        total = total + (pltpu.roll(value, 1, 1) + pltpu.roll(value, width - 1, 1))
        total = total + (pltpu.roll(value, 1, 2) + pltpu.roll(value, cy - 1, 2))
        value = (total + centre * value) * scale
    low = lax.broadcasted_iota(i32, (nz, width // 2, cy), 1) < half
    out[...] = pltpu.roll(jnp.where(low, value[:, width // 2 :], value[:, : width // 2]), half, 1)


def strip_kernel(
    inside, strips, got_even, got_odd, buffer, got, out, daughters, merged, taken, semaphores,
    *, grid_count, row_count, capacity, step,
):
    taken[...] = take_in(
        buffer[...], got[...], (lax.axis_index("gx") // step) % 2 == 1, capacity * step
    )
    copies = [pltpu.make_async_copy(taken, daughters, semaphores.at[0])]
    copies[0].start()
    nz, cx, cy = inside.shape
    m = strips.shape[1]
    width = m // nz
    g, h = lax.axis_index("gx"), lax.axis_index("gy")
    h_even = h % 2 == 0
    edge = 2 * sweeps
    has_right, has_left = h + 1 < row_count, h >= 1
    a, b = got_even[...], got_odd[...]
    right = jnp.where(has_right, jnp.where(h_even, a, b), 0.0)
    left = jnp.where(has_left, jnp.where(h_even, b, a), 0.0)
    own = strips[...]
    tiles = m // LANES
    bands = [
        jnp.concatenate([rows[:, k * LANES : (k + 1) * LANES] for rows in (left, own, right)], axis=0) for k in range(tiles)
    ]
    shape = bands[0].shape
    count = shape[0]
    lane = lax.broadcasted_iota(i32, shape, 1)
    line = lax.broadcasted_iota(i32, shape, 0)
    outside = (line < sweeps) & jnp.logical_not(has_left) | (line >= count - sweeps) & jnp.logical_not(has_right)
    at_x = lane % width
    outside = outside | (g == 0) & (at_x < cx // 2) | (g == grid_count - 1) & (at_x >= width - cx // 2)
    scale = jnp.where(outside, 0.0, diffusion_number)
    z_first, z_last = lane < width, lane >= LANES - width
    centre = 1.0 / diffusion_number - 6.0
    for turn in range(sweeps):
        wrapped = jnp.where(z_first, 0.0, pltpu.roll(bands[-1], width, 1))
        onward = jnp.where(z_last, 0.0, pltpu.roll(bands[0], LANES - width, 1))
        around = [wrapped] + bands + [onward]
        bands = [
            (
                (around[k] + around[k + 2])
                + (pltpu.roll(b, 1, 0) + pltpu.roll(b, count - 1, 0))
                + (pltpu.roll(b, 1, 1) + pltpu.roll(b, LANES - 1, 1))
                + centre * b
            ) * scale
            for k, b in enumerate(bands)
        ]
    placed = lax.broadcasted_iota(i32, (edge, cy), 0)
    placed = jnp.where(placed < sweeps, placed, placed + cy - edge)
    placer = (placed == lax.broadcasted_iota(i32, (edge, cy), 1)).astype(f32)
    placers = jnp.concatenate([placer, placer], axis=0).astype(bf16)
    planes = nz // tiles
    low = lax.broadcasted_iota(i32, (planes, cx, cy), 1) < cx // 2
    at_y = lax.broadcasted_iota(i32, (planes, cx, cy), 2)
    rim = (at_y < sweeps) | (at_y >= cy - sweeps)
    for k, b in enumerate(bands):
        final = jnp.concatenate([b[sweeps : 2 * sweeps], b[count - 2 * sweeps : count - sweeps]], axis=0)
        high = final.astype(bf16).astype(f32)
        stacked = jnp.concatenate([high, final - high], axis=0).astype(bf16)
        edges = lax.dot_general(
            stacked, placers, (((0,), (0,)), ((), ())), preferred_element_type=f32
        ).reshape(planes, width, cy)
        mixed = pltpu.roll(jnp.where(low, edges[:, cx:], edges[:, :cx]), cx // 2, 1)
        for at in range(planes):
            z = at * tiles + k
            merged[k, at] = jnp.where(rim[at], mixed[at], inside[z])
        copies.append(pltpu.make_async_copy(merged.at[k], out.at[:, k], semaphores.at[k + 1]))
        copies[-1].start()
    for copy in copies:
        copy.wait()


def pieces(value):
    high = value.astype(bf16)
    rest = value - high.astype(f32)
    middle = rest.astype(bf16)
    return high, middle, (rest - middle.astype(f32)).astype(bf16)


PIECE_ROWS = 48


def put_pieces(message, at, value):
    for number, piece in enumerate(pieces(value)[:2]):
        start = at + number * PIECE_ROWS
        message[start : start + value.shape[0], :] = piece


def get_pieces(message, at, count):
    starts = [at + number * PIECE_ROWS for number in range(2)]
    return sum(message[start : start + count, :].astype(f32) for start in starts)


def first_send(buffer, mine, width):
    count = buffer.shape[1]
    half = count // 2
    left, right = buffer[:, :half], buffer[:, half:]
    if width == half:
        return jnp.where(mine, left, right)
    bit = (lax.broadcasted_iota(i32, left.shape, 1) // width) % 2 == 1
    moved = jnp.where(mine, pltpu.roll(right, width, 1), pltpu.roll(right, half - width, 1))
    return jnp.where(jnp.logical_xor(bit, mine), left, moved)


def take_in(buffer, got, mine, width):
    count = buffer.shape[1]
    half = count // 2
    left, right = buffer[:, :half], buffer[:, half:]
    if width == half:
        left, right = jnp.where(mine, got, left), jnp.where(mine, right, got)
    else:
        bit = (lax.broadcasted_iota(i32, left.shape, 1) // width) % 2 == 1
        other = jnp.logical_xor(bit, mine)
        moved = jnp.where(mine, pltpu.roll(got, half - width, 1), pltpu.roll(got, width, 1))
        left, right = jnp.where(other, moved, left), jnp.where(other, got, right)
    return jnp.concatenate([left, right], axis=1)


def place_columns(target, capacity, columns):
    picks = target.shape[1]
    square = (picks, picks)
    across = jnp.broadcast_to(target, square)
    down = jnp.broadcast_to(column(target, picks), square)
    earlier = lax.broadcasted_iota(i32, square, 0) < lax.broadcasted_iota(i32, square, 1)
    rank = jnp.sum(jnp.where((across == down) & earlier, 1, 0), axis=0, keepdims=True)
    position = target * capacity + rank
    return (lax.broadcasted_iota(i32, (columns, picks), 0) == position).astype(f32).astype(bf16)


def relay_kernel(buffer, got, merged, send, *, capacity, step, after):
    g = lax.axis_index("gx")
    value = take_in(buffer[...], got[...], (g // step) % 2 == 1, capacity * step)
    merged[...] = value
    send[...] = first_send(value, (g // after) % 2 == 1, capacity * after)


def solution(mesh):
    grid_count, row_count = mesh.shape["gx"], mesh.shape["gy"]

    def swap(value, partner):
        return lax.ppermute(value, GRID, swap_pairs(grid_count, row_count, partner))

    def side_odd(g, h):
        p = h + 1 if h % 2 else h - 1
        return (g, p) if 0 <= p < row_count else (g, h ^ (row_count - 1))

    def shards(
        cell_state, coupling, basal_rate, half_sat, decay_rate, uptake_weight,
        agent_counts, divider_ids, destinations, voxel_index, oxygen,
    ):
        species, agents = cell_state.shape
        nz, cx, cy = oxygen.shape
        picks = divider_ids.shape[0]
        rows = agents // LANES
        head = nz // 2 * cx
        capacity = max(2, 2 * picks // grid_count)
        columns = grid_count * capacity

        def line(value):
            return value.reshape(1, -1)

        def kernel(body, **sizes):
            def run(*refs):
                return body(*refs, **sizes)

            return run

        m = nz * cx
        count = 3 * rows
        pieces_rows = 2 * PIECE_ROWS
        one_field = (nz, 2 * cx, cy)
        listed = (count, LANES)
        half_buffer = ((species, columns // 2), f32)
        assert species <= PIECE_ROWS and columns == 2 * LANES and grid_count >= 8

        state, message_even, message_odd, listing, buffer = call(
            kernel(advance_kernel, cy=cy, cx=cx, nz=nz, capacity=capacity),
            [((species, agents), f32), ((head + count + pieces_rows, LANES), bf16), ((head + count, LANES), bf16),
             (listed, bf16), ((species, columns), f32)],
            "advance",
            [agent_counts, cell_state, coupling, line(basal_rate), line(half_sat), line(decay_rate),
             line(uptake_weight), voxel_index.reshape(rows, LANES), oxygen, line(divider_ids), line(destinations)],
            smem=(0,),
            hbm=range(1, 11),
            scratch=[pltpu.VMEM((species, agents), f32), pltpu.VMEM((species, species), f32)]
            + [pltpu.VMEM((1, species), f32)] * 4
            + [pltpu.VMEM((rows, LANES), i32), pltpu.VMEM((nz, cx, cy), f32)]
            + [pltpu.VMEM((1, picks), i32)] * 2
            + [pltpu.VMEM((rows, LANES), f32), pltpu.VMEM((species, 3 * PIECE_ROWS), bf16),
               pltpu.VMEM((3 * PIECE_ROWS, agents), bf16), pltpu.VMEM((agents, picks), bf16),
               pltpu.VMEM((2 * rows, LANES), f32), pltpu.SemaphoreType.DMA((10,))],
        )
        near_e = swap(message_even, near_even)
        near_o = swap(message_odd, near_odd)
        base, new_state = call(
            own_kernel,
            [(one_field, f32), ((species, agents), f32)],
            "own",
            [oxygen, listing, state],
            hbm=(0, 4),
            scratch=[pltpu.VMEM((1,) + listed, f32), pltpu.VMEM((m, agents), bf16), pltpu.VMEM((2 * cy, agents), bf16),
                     pltpu.VMEM((nz, cx, cy), f32), pltpu.SemaphoreType.DMA((2,))],
        )
        buffer, base = lax.optimization_barrier((buffer, base))
        buffer, message_far = call(
            kernel(relay_first_kernel, capacity=capacity, head=head),
            [((species, columns), f32), ((count + pieces_rows, LANES), bf16)],
            "relay",
            [buffer, near_e, listing],
        )
        far_e = swap(message_far, far_even)
        far_o = swap(listing, far_odd)
        base, _ = lax.optimization_barrier((base, message_far))
        (field,) = call(
            kernel(near_kernel, grid_count=grid_count),
            [(one_field, f32)],
            "near",
            [base, listing, near_e, near_o],
            scratch=[pltpu.VMEM((2,) + listed, f32), pltpu.VMEM((m, 2 * agents), bf16),
                     pltpu.VMEM((2 * cy, 2 * agents), bf16)],
        )
        step = 4
        field, strips, strip_even, strip_odd, buffer, send = call(
            kernel(far_kernel, grid_count=grid_count, capacity=capacity, after=step),
            [(one_field, f32), ((4 * sweeps, 2 * m), f32), ((sweeps, 2 * m), f32), ((sweeps, 2 * m), f32),
             ((species, columns), f32)] + [half_buffer],
            "far",
            [field, buffer, near_e, near_o, far_e, far_o],
            scratch=[pltpu.VMEM((2,) + listed, f32), pltpu.VMEM((head // 2, 2 * agents), bf16),
                     pltpu.VMEM((2 * cy, 2 * agents), bf16)],
        )
        got = swap(send, lambda g, h: (g ^ step, h))
        got_odd = swap(strip_odd, side_odd)
        got_even = swap(strip_even, side_even)
        (inside,) = call(
            kernel(sweep_kernel, grid_count=grid_count), [((nz, cx, cy), f32)], "sweeps", [field]
        )
        while step < grid_count // 2:
            after = 2 * step
            buffer, sent = call(
                kernel(relay_kernel, capacity=capacity, step=step, after=after),
                [((species, columns), f32), half_buffer],
                "relay",
                [buffer, got],
            )
            step = after
            got = swap(sent, lambda g, h: (g ^ step, h))
        tiles = 2 * m // LANES
        new_oxygen, daughter_state = call(
            kernel(strip_kernel, grid_count=grid_count, row_count=row_count, capacity=capacity, step=step),
            [((nz // tiles, tiles, cx, cy), f32), ((species, columns), f32)],
            "strips",
            [inside, strips, got_even, got_odd, buffer, got],
            hbm=(6, 7),
            scratch=[pltpu.VMEM((tiles, nz // tiles, cx, cy), f32), pltpu.VMEM((species, columns), f32),
                     pltpu.SemaphoreType.DMA((tiles + 1,))],
        )
        return new_state, daughter_state, new_oxygen.reshape(nz, cx, cy)

    return jax.shard_map(
        shards,
        mesh=mesh,
        in_specs=(
            P(None, GRID), P(), P(), P(), P(), P(), P(GRID), P(GRID), P(GRID, None), P(GRID), P(None, "gx", "gy"),
        ),
        out_specs=(P(None, GRID), P(None, GRID), P(None, "gx", "gy")),
        check_vma=False,
    )
```

```python
import jax
import jax.numpy as jnp
from jax import lax
from jax.experimental import pallas as pl
from jax.experimental.pallas import tpu as pltpu
from jax.sharding import PartitionSpec as P

time_step = 0.25
diffusion_number = 0.16
sweeps = 4
GRID = ("gx", "gy")
LANES = 128
EXACT = lax.Precision.HIGHEST
f32, bf16, i32 = jnp.float32, jnp.bfloat16, jnp.int32
VMEM_LIMIT = 48 << 20


def call(body, outs, name, inputs, smem=(), hbm=(), scratch=(), cost=None):
    def spec(at, shape):
        if at in smem:
            return pl.BlockSpec(memory_space=pltpu.SMEM)
        return pl.BlockSpec(memory_space=pltpu.HBM) if at in hbm else pl.BlockSpec(memory_space=pltpu.VMEM)

    count = len(inputs)
    inputs = [pltpu.with_memory_space_constraint(v, pltpu.HBM) if at in hbm else v for at, v in enumerate(inputs)]
    return pl.pallas_call(
        body,
        out_shape=tuple(jax.ShapeDtypeStruct(s, t) for s, t in outs),
        in_specs=[spec(at, value.shape) for at, value in enumerate(inputs)],
        out_specs=tuple(spec(count + at, s) for at, (s, t) in enumerate(outs)),
        scratch_shapes=scratch,
        compiler_params=pltpu.CompilerParams(vmem_limit_bytes=VMEM_LIMIT),
        name=name,
    )(*inputs)


def swap_pairs(grid_count, row_count, partner):
    pairs = []
    for g in range(grid_count):
        for h in range(row_count):
            p, q = partner(g, h)
            if not (0 <= p < grid_count and 0 <= q < row_count):
                p, q = g, h ^ 1
            pairs.append((g * row_count + h, p * row_count + q))
    return pairs


def near_even(g, h):
    return g ^ 1, h


def near_odd(g, h):
    return (g + 1 if g % 2 else g - 1), h


def far_even(g, h):
    return g ^ 2, h


def far_odd(g, h):
    return (g + 2 if g & 2 else g - 2), h


def side_even(g, h):
    return g, h ^ 1


def column(row, count):
    shape = (count, count)
    same = lax.broadcasted_iota(i32, shape, 0) == lax.broadcasted_iota(i32, shape, 1)
    return jnp.sum(jnp.where(same, jnp.broadcast_to(row, shape), 0), axis=1, keepdims=True)


def advance_kernel(
    count_ref, cell_hbm, coupling_hbm, basal_hbm, half_hbm, decay_hbm, weight_hbm, voxel_hbm, oxygen_hbm, ids_hbm,
    targets_hbm, new_state, message_even, message_odd, message_far, buffer,
    cell, coupling, basal, half, decay, weight, voxel, oxygen, ids, targets, drive, matrices, stack, chosen, codes, semaphores,
    *, cy, cx, nz, capacity,
):
    pairs = (
        (ids_hbm, ids), (voxel_hbm, voxel), (targets_hbm, targets), (coupling_hbm, coupling), (basal_hbm, basal),
        (half_hbm, half), (decay_hbm, decay), (weight_hbm, weight), (cell_hbm, cell), (oxygen_hbm, oxygen),
    )
    species, agents = cell.shape
    copies = [pltpu.make_async_copy(a, b, semaphores.at[i]) for i, (a, b) in enumerate(pairs)]
    for copy in copies:
        copy.start()
    stack[...] = jnp.zeros_like(stack)
    for copy in copies[:-2]:
        copy.wait()
    rows = agents // LANES
    picks = ids.shape[1]
    chosen[...] = (lax.broadcasted_iota(i32, (agents, picks), 0) == ids[...]).astype(f32).astype(bf16)
    code = voxel[...]
    at_y = code % cy
    at_x = (code // cy) % cx
    at_z = (code // (cy * cx)) % nz
    slab_x = (code // (cy * cx * nz)) * cx + at_x + cx // 2
    codes[:rows, :] = (at_z * cx + slab_x % cx - nz * cx // 2).astype(f32)
    codes[rows:, :] = ((slab_x // cx) * cy + at_y - 2 * cy).astype(f32)
    basal_c, half_c, decay_c, weight_c = (column(r[...], species) for r in (basal, half, decay, weight))
    half_square = half_c * half_c
    matrix_high, matrix_low, _ = pieces(coupling[...])
    matrices[...] = jnp.zeros_like(matrices)
    for number, piece in enumerate((matrix_high, matrix_high, matrix_low)):
        matrices[:, number * PIECE_ROWS : number * PIECE_ROWS + species] = piece
    matrix = matrices[...]

    def rates(current):
        square = current * current
        occupancy = square / (half_square + square)
        high = occupancy.astype(bf16)
        low = (occupancy - high.astype(f32)).astype(bf16)
        for number, piece in enumerate((high, low, high)):
            stack[number * PIECE_ROWS : number * PIECE_ROWS + species, :] = piece
        drive_sum = jnp.dot(matrix, stack[...], preferred_element_type=f32)
        return basal_c + drive_sum - decay_c * current

    placing = place_columns(targets[...], capacity, buffer.shape[1])
    copies[-2].wait()
    current = cell[...]
    for substep in range(2):
        middle = current + (0.5 * time_step) * rates(current)
        current = current + time_step * rates(middle)
    new_state[...] = current
    total = jnp.sum(weight_c * current, axis=0, keepdims=True)
    for c in range(rows):
        drive[c : c + 1, :] = total[:, c * LANES : (c + 1) * LANES]
    mothers = sum(jnp.dot(p, chosen[...], preferred_element_type=f32) for p in pieces(current)[:2])
    copies[-1].wait()
    x = drive[...]
    soft = jnp.maximum(x, 0.0) + jnp.log1p(jnp.exp(-jnp.abs(x)))
    slot = lax.broadcasted_iota(i32, (rows, LANES), 0) * LANES + lax.broadcasted_iota(i32, (rows, LANES), 1)
    uptake = jnp.where(slot < count_ref[0], soft, 0.0)
    listing = jnp.concatenate([uptake, codes[...]], axis=0).astype(bf16)
    own = oxygen[...] - 1.0
    turned = pltpu.roll(own, cx // 2, 1)
    low = lax.broadcasted_iota(i32, (nz // 2, cx, cy), 1) < cx // 2
    a, b = own[: nz // 2], own[nz // 2 :]
    ta, tb = turned[: nz // 2], turned[nz // 2 :]
    upper = jnp.where(low, ta, b)
    lower = jnp.where(low, a, tb)
    even = lax.axis_index("gx") % 2 == 0
    to_next = upper.reshape(nz // 2 * cx, cy)
    to_previous = lower.reshape(nz // 2 * cx, cy)
    head = nz // 2 * cx
    message_even[:head, :] = jnp.where(even, to_next, to_previous).astype(bf16)
    message_odd[:head, :] = jnp.where(even, to_previous, to_next).astype(bf16)
    tail = head + 3 * rows
    message_even[head:tail, :] = listing
    message_odd[head:, :] = listing
    message_far[...] = listing
    placed = sum(product(p, placing) for p in pieces(mothers)[:2])
    buffer[...] = placed
    put_pieces(message_even, tail, first_send(placed, lax.axis_index("gx") % 2 == 1, capacity))


def one_hots(lists, which, first, m, base, width, left, right, slot):
    rows = lists.shape[1] // 3
    pack = 16
    row_at = (lax.broadcasted_iota(i32, (m, LANES), 0) + first).astype(f32).astype(bf16).reshape(m // pack, pack, LANES)
    col_at = (lax.broadcasted_iota(i32, (width, LANES), 0) + base).astype(f32).astype(bf16)
    col_at = col_at.reshape(width // pack, pack, LANES)
    one, zero = jnp.ones((), bf16), jnp.zeros((), bf16)

    def line(at):
        return jnp.broadcast_to(lists[which, at : at + 1, :], (pack, LANES)).astype(bf16)[None]

    for at in range(rows):
        columns = slice((slot * rows + at) * LANES, (slot * rows + at + 1) * LANES)
        hit = jnp.where(row_at == line(rows + at), one, zero)
        left[:, columns] = hit.reshape(m, LANES)
        spread = jnp.where(col_at == line(2 * rows + at), jnp.broadcast_to(line(at), col_at.shape), zero)
        right[:width, columns] = spread.reshape(width, LANES)


def product(left, right):
    return lax.dot_general(left, right, (((1,), (1,)), ((), ())), preferred_element_type=f32)


def own_kernel(oxygen_hbm, own_list, state, base, new_state, lists, left, right, oxygen, semaphores):
    copy = pltpu.make_async_copy(oxygen_hbm, oxygen, semaphores.at[0])
    copy.start()
    store = pltpu.make_async_copy(state, new_state, semaphores.at[1])
    store.start()
    nz, cx, cy = oxygen.shape
    m = nz * cx
    lists[0] = own_list[...].astype(f32)
    one_hots(lists, 0, -m // 2, m, -cy, 2 * cy, left, right, 0)
    total = product(left[...], right[...])
    copy.wait()
    low = lax.broadcasted_iota(i32, (nz, cx, cy), 1) < cx // 2
    inner = pltpu.roll(oxygen[...], cx // 2, 1)
    base[:, :cx, :] = jnp.where(low, 0.0, inner) - total[:, :cy].reshape(nz, cx, cy)
    base[:, cx:, :] = jnp.where(low, inner, 0.0) - total[:, cy:].reshape(nz, cx, cy)
    store.wait()


def keep(listing, rows, valid):
    index = lax.broadcasted_iota(i32, listing.shape, 0)
    return jnp.where((index < rows) & jnp.logical_not(valid), 0.0, listing)


def relay_first_kernel(buffer, got, listing, merged, message, *, capacity, head):
    g = lax.axis_index("gx")
    species = buffer.shape[0]
    count = listing.shape[0]
    value = take_in(buffer[...], get_pieces(got, head + count, species), g % 2 == 1, capacity)
    merged[...] = value
    message[:count, :] = listing[...]
    put_pieces(message, count, first_send(value, (g // 2) % 2 == 1, 2 * capacity))


def near_kernel(base, listing, near_e, near_o, field, lists, left, right, *, grid_count):
    nz, cx, cy = base.shape[0], base.shape[1] // 2, base.shape[2]
    m, head = nz * cx, nz // 2 * cx
    count = listing.shape[0]
    rows = count // 3
    g = lax.axis_index("gx")
    even = g % 2 == 0
    e, o = near_e[head : head + count, :].astype(f32), near_o[head : head + count, :].astype(f32)
    lists[0] = keep(jnp.where(even, e, o), rows, g + 1 < grid_count)
    lists[1] = keep(jnp.where(even, o, e), rows, g >= 1)
    one_hots(lists, 0, -m // 2, m, -2 * cy, 2 * cy, left, right, 0)
    one_hots(lists, 1, -m // 2, m, 0, 2 * cy, left, right, 1)
    total = product(left[...], right[...])
    field[:, :cx, :] = base[:, :cx, :] - total[:, :cy].reshape(nz, cx, cy)
    field[:, cx:, :] = base[:, cx:, :] - total[:, cy:].reshape(nz, cx, cy)


def far_kernel(
    base, buffer, near_e, near_o, far_e, far_o, field, strips, strip_even, strip_odd, merged, send,
    lists, left, right, *, grid_count, capacity, after,
):
    nz, cx, cy = base.shape[0], base.shape[1] // 2, base.shape[2]
    half, zh = cx // 2, nz // 2
    head, m = zh * cx, nz * cx
    count = far_o.shape[0]
    rows = count // 3
    agents = rows * LANES
    g = lax.axis_index("gx")
    even = g % 2 == 0
    low_pair = g % 4 < 2
    fe, fo = far_e[:count, :].astype(f32), far_o[...].astype(f32)
    quarter = zh // 2
    for which, listing, base_code, valid in (
        (0, jnp.where(low_pair, fe, fo), -2 * cy, g + 2 < grid_count),
        (1, jnp.where(low_pair, fo, fe), cy, g >= 2),
    ):
        code = listing[rows : 2 * rows].astype(i32) + m // 2
        at_z, at_y = code // cx, listing[2 * rows :].astype(i32) - base_code
        inner_z = at_z % zh
        code = (inner_z % quarter) * cx + (inner_z // quarter) * half + code % half
        lists[which, :rows] = jnp.where(valid, listing[:rows], 0.0)
        lists[which, rows : 2 * rows] = code.astype(f32)
        lists[which, 2 * rows :] = jnp.where((at_y >= 0) & (at_y < cy), (at_z // zh) * cy + at_y, -1).astype(f32)
    one_hots(lists, 0, 0, head // 2, 0, 2 * cy, left, right, 0)
    one_hots(lists, 1, 0, head // 2, 0, 2 * cy, left, right, 1)
    low_quarter = lax.broadcasted_iota(i32, (quarter, cx, cy), 1) < half

    def unfold(total):
        lower, upper = (total[:, t * cy : (t + 1) * cy].reshape(quarter, cx, cy) for t in range(2))
        return jnp.concatenate(
            [
                jnp.where(low_quarter, lower, pltpu.roll(upper, half, 1)),
                jnp.where(low_quarter, pltpu.roll(lower, half, 1), upper),
            ],
            axis=0,
        )

    past_after = unfold(product(left[:, :agents], right[:, :agents]))
    past_before = unfold(product(left[:, agents:], right[:, agents:]))

    e, o = near_e[:head, :].astype(f32), near_o[:head, :].astype(f32)
    shape = (zh, cx, cy)
    from_before = jnp.where(g >= 1, jnp.where(even, o, e) + 1.0, 0.0).reshape(shape) - past_before
    from_after = jnp.where(g + 1 < grid_count, jnp.where(even, e, o) + 1.0, 0.0).reshape(shape) - past_after
    low = lax.broadcasted_iota(i32, shape, 1) < half
    field[:zh, :cx] = base[:zh, :cx] + jnp.where(low, from_before, 0.0)
    field[zh:, :cx] = base[zh:, :cx] + jnp.where(low, pltpu.roll(from_before, half, 1), 0.0)
    field[:zh, cx:] = base[:zh, cx:] + jnp.where(low, 0.0, pltpu.roll(from_after, half, 1))
    field[zh:, cx:] = base[zh:, cx:] + jnp.where(low, 0.0, from_after)

    edge = 2 * sweeps
    picked = lax.broadcasted_iota(i32, (2 * edge, cy), 0)
    picked = jnp.where(picked < edge, picked, picked + cy - 2 * edge)
    picker = (picked == lax.broadcasted_iota(i32, (2 * edge, cy), 1)).astype(f32).astype(bf16)
    tiles = 2 * m // LANES
    value = field[...].reshape(nz // tiles, tiles, 2 * cx, cy)
    flat = jnp.concatenate([value[:, k].reshape(LANES, cy) for k in range(tiles)], axis=0)
    rims = product(jnp.concatenate([picker, picker], axis=1), jnp.concatenate(pieces(flat)[:2], axis=1))
    strips[...] = rims
    h_even = lax.axis_index("gy") % 2 == 0
    head_rows, tail_rows = rims[:sweeps], rims[2 * edge - sweeps :]
    strip_even[...] = jnp.where(h_even, tail_rows, head_rows)
    strip_odd[:sweeps, :] = jnp.where(h_even, head_rows, tail_rows)
    strip_odd[sweeps:, :] = head_rows
    value = take_in(buffer[...], get_pieces(far_e, count, buffer.shape[0]), (g // 2) % 2 == 1, 2 * capacity)
    merged[...] = value
    send[...] = first_send(value, (g // after) % 2 == 1, after * capacity)


def sweep_kernel(field, out, *, grid_count):
    nz, width, cy = field.shape
    half = width // 4
    g = lax.axis_index("gx")
    at_x = lax.broadcasted_iota(i32, (nz, width, cy), 1)
    outside = (g == 0) & (at_x < half) | (g == grid_count - 1) & (at_x >= width - half)
    scale = jnp.where(outside, 0.0, diffusion_number)
    centre = 1.0 / diffusion_number - 6.0
    plane = jnp.zeros((1, width, cy), f32)
    value = field[...]
    for turn in range(sweeps):
        total = jnp.concatenate([plane, value[:-1]], axis=0) + jnp.concatenate([value[1:], plane], axis=0)
        total = total + (pltpu.roll(value, 1, 1) + pltpu.roll(value, width - 1, 1))
        total = total + (pltpu.roll(value, 1, 2) + pltpu.roll(value, cy - 1, 2))
        value = (total + centre * value) * scale
    low = lax.broadcasted_iota(i32, (nz, width // 2, cy), 1) < half
    out[...] = pltpu.roll(jnp.where(low, value[:, width // 2 :], value[:, : width // 2]), half, 1)


def strip_kernel(
    inside, strips, got_even, got_odd, buffer, got, out, daughters, merged, taken, semaphores,
    *, grid_count, row_count, capacity, step,
):
    taken[...] = take_in(
        buffer[...], got[...], (lax.axis_index("gx") // step) % 2 == 1, capacity * step
    )
    copies = [pltpu.make_async_copy(taken, daughters, semaphores.at[0])]
    copies[0].start()
    nz, cx, cy = inside.shape
    m = strips.shape[1]
    width = m // nz
    g, h = lax.axis_index("gx"), lax.axis_index("gy")
    h_even = h % 2 == 0
    edge = 2 * sweeps
    has_right, has_left = h + 1 < row_count, h >= 1
    a, b = got_even[...], got_odd[:sweeps, :]
    right = jnp.where(has_right, jnp.where(h_even, a, b), 0.0)
    left = jnp.where(has_left, jnp.where(h_even, b, a), 0.0)
    own = strips[...]
    tiles = m // LANES
    bands = [
        jnp.concatenate([rows[:, k * LANES : (k + 1) * LANES] for rows in (left, own, right)], axis=0) for k in range(tiles)
    ]
    shape = bands[0].shape
    count = shape[0]
    lane = lax.broadcasted_iota(i32, shape, 1)
    line = lax.broadcasted_iota(i32, shape, 0)
    outside = (line < sweeps) & jnp.logical_not(has_left) | (line >= count - sweeps) & jnp.logical_not(has_right)
    at_x = lane % width
    outside = outside | (g == 0) & (at_x < cx // 2) | (g == grid_count - 1) & (at_x >= width - cx // 2)
    scale = jnp.where(outside, 0.0, diffusion_number)
    z_first, z_last = lane < width, lane >= LANES - width
    centre = 1.0 / diffusion_number - 6.0
    for turn in range(sweeps):
        wrapped = jnp.where(z_first, 0.0, pltpu.roll(bands[-1], width, 1))
        onward = jnp.where(z_last, 0.0, pltpu.roll(bands[0], LANES - width, 1))
        around = [wrapped] + bands + [onward]
        bands = [
            (
                (around[k] + around[k + 2])
                + (pltpu.roll(b, 1, 0) + pltpu.roll(b, count - 1, 0))
                + (pltpu.roll(b, 1, 1) + pltpu.roll(b, LANES - 1, 1))
                + centre * b
            ) * scale
            for k, b in enumerate(bands)
        ]
    placed = lax.broadcasted_iota(i32, (edge, cy), 0)
    placed = jnp.where(placed < sweeps, placed, placed + cy - edge)
    placer = (placed == lax.broadcasted_iota(i32, (edge, cy), 1)).astype(f32)
    placers = jnp.concatenate([placer, placer], axis=0).astype(bf16)
    planes = nz // tiles
    low = lax.broadcasted_iota(i32, (planes, cx, cy), 1) < cx // 2
    at_y = lax.broadcasted_iota(i32, (planes, cx, cy), 2)
    rim = (at_y < sweeps) | (at_y >= cy - sweeps)
    for k, b in enumerate(bands):
        final = jnp.concatenate([b[sweeps : 2 * sweeps], b[count - 2 * sweeps : count - sweeps]], axis=0)
        high = final.astype(bf16).astype(f32)
        stacked = jnp.concatenate([high, final - high], axis=0).astype(bf16)
        edges = lax.dot_general(
            stacked, placers, (((0,), (0,)), ((), ())), preferred_element_type=f32
        ).reshape(planes, width, cy)
        mixed = pltpu.roll(jnp.where(low, edges[:, cx:], edges[:, :cx]), cx // 2, 1)
        for at in range(planes):
            z = at * tiles + k
            merged[k, at] = jnp.where(rim[at], mixed[at], inside[z])
        copies.append(pltpu.make_async_copy(merged.at[k], out.at[:, k], semaphores.at[k + 1]))
        copies[-1].start()
    for copy in copies:
        copy.wait()


def pieces(value):
    high = value.astype(bf16)
    rest = value - high.astype(f32)
    middle = rest.astype(bf16)
    return high, middle, (rest - middle.astype(f32)).astype(bf16)


PIECE_ROWS = 48


def put_pieces(message, at, value):
    for number, piece in enumerate(pieces(value)[:2]):
        start = at + number * PIECE_ROWS
        message[start : start + value.shape[0], :] = piece


def get_pieces(message, at, count):
    starts = [at + number * PIECE_ROWS for number in range(2)]
    return sum(message[start : start + count, :].astype(f32) for start in starts)


def first_send(buffer, mine, width):
    count = buffer.shape[1]
    half = count // 2
    left, right = buffer[:, :half], buffer[:, half:]
    if width == half:
        return jnp.where(mine, left, right)
    bit = (lax.broadcasted_iota(i32, left.shape, 1) // width) % 2 == 1
    moved = jnp.where(mine, pltpu.roll(right, width, 1), pltpu.roll(right, half - width, 1))
    return jnp.where(jnp.logical_xor(bit, mine), left, moved)


def take_in(buffer, got, mine, width):
    count = buffer.shape[1]
    half = count // 2
    left, right = buffer[:, :half], buffer[:, half:]
    if width == half:
        left, right = jnp.where(mine, got, left), jnp.where(mine, right, got)
    else:
        bit = (lax.broadcasted_iota(i32, left.shape, 1) // width) % 2 == 1
        other = jnp.logical_xor(bit, mine)
        moved = jnp.where(mine, pltpu.roll(got, half - width, 1), pltpu.roll(got, width, 1))
        left, right = jnp.where(other, moved, left), jnp.where(other, got, right)
    return jnp.concatenate([left, right], axis=1)


def place_columns(target, capacity, columns):
    picks = target.shape[1]
    square = (picks, picks)
    across = jnp.broadcast_to(target, square)
    down = jnp.broadcast_to(column(target, picks), square)
    earlier = lax.broadcasted_iota(i32, square, 0) < lax.broadcasted_iota(i32, square, 1)
    rank = jnp.sum(jnp.where((across == down) & earlier, 1, 0), axis=0, keepdims=True)
    position = target * capacity + rank
    return (lax.broadcasted_iota(i32, (columns, picks), 0) == position).astype(f32).astype(bf16)


def relay_kernel(buffer, got, merged, send, *, capacity, step, after):
    g = lax.axis_index("gx")
    value = take_in(buffer[...], got[...], (g // step) % 2 == 1, capacity * step)
    merged[...] = value
    send[...] = first_send(value, (g // after) % 2 == 1, capacity * after)


def solution(mesh):
    grid_count, row_count = mesh.shape["gx"], mesh.shape["gy"]

    def swap(value, partner):
        return lax.ppermute(value, GRID, swap_pairs(grid_count, row_count, partner))

    def side_odd(g, h):
        p = h + 1 if h % 2 else h - 1
        return (g, p) if 0 <= p < row_count else (g, h ^ (row_count - 1))

    def shards(
        cell_state, coupling, basal_rate, half_sat, decay_rate, uptake_weight,
        agent_counts, divider_ids, destinations, voxel_index, oxygen,
    ):
        species, agents = cell_state.shape
        nz, cx, cy = oxygen.shape
        picks = divider_ids.shape[0]
        rows = agents // LANES
        head = nz // 2 * cx
        capacity = max(2, 2 * picks // grid_count)
        columns = grid_count * capacity

        def line(value):
            return value.reshape(1, -1)

        def kernel(body, **sizes):
            def run(*refs):
                return body(*refs, **sizes)

            return run

        m = nz * cx
        count = 3 * rows
        pieces_rows = 2 * PIECE_ROWS
        one_field = (nz, 2 * cx, cy)
        listed = (count, LANES)
        half_buffer = ((species, columns // 2), f32)
        assert species <= PIECE_ROWS and columns == 2 * LANES and grid_count >= 8

        state, message_even, message_odd, listing, buffer = call(
            kernel(advance_kernel, cy=cy, cx=cx, nz=nz, capacity=capacity),
            [((species, agents), f32), ((head + count + pieces_rows, LANES), bf16), ((head + count, LANES), bf16),
             (listed, bf16), ((species, columns), f32)],
            "advance",
            [agent_counts, cell_state, coupling, line(basal_rate), line(half_sat), line(decay_rate),
             line(uptake_weight), voxel_index.reshape(rows, LANES), oxygen, line(divider_ids), line(destinations)],
            smem=(0,),
            hbm=range(1, 11),
            scratch=[pltpu.VMEM((species, agents), f32), pltpu.VMEM((species, species), f32)]
            + [pltpu.VMEM((1, species), f32)] * 4
            + [pltpu.VMEM((rows, LANES), i32), pltpu.VMEM((nz, cx, cy), f32)]
            + [pltpu.VMEM((1, picks), i32)] * 2
            + [pltpu.VMEM((rows, LANES), f32), pltpu.VMEM((species, 3 * PIECE_ROWS), bf16),
               pltpu.VMEM((3 * PIECE_ROWS, agents), bf16), pltpu.VMEM((agents, picks), bf16),
               pltpu.VMEM((2 * rows, LANES), f32), pltpu.SemaphoreType.DMA((10,))],
        )
        near_e = swap(message_even, near_even)
        near_o = swap(message_odd, near_odd)
        base, new_state = call(
            own_kernel,
            [(one_field, f32), ((species, agents), f32)],
            "own",
            [oxygen, listing, state],
            hbm=(0, 4),
            scratch=[pltpu.VMEM((1,) + listed, f32), pltpu.VMEM((m, agents), bf16), pltpu.VMEM((2 * cy, agents), bf16),
                     pltpu.VMEM((nz, cx, cy), f32), pltpu.SemaphoreType.DMA((2,))],
        )
        buffer, base = lax.optimization_barrier((buffer, base))
        buffer, message_far = call(
            kernel(relay_first_kernel, capacity=capacity, head=head),
            [((species, columns), f32), ((count + pieces_rows, LANES), bf16)],
            "relay",
            [buffer, near_e, listing],
        )
        far_e = swap(message_far, far_even)
        far_o = swap(listing, far_odd)
        base, _ = lax.optimization_barrier((base, message_far))
        (field,) = call(
            kernel(near_kernel, grid_count=grid_count),
            [(one_field, f32)],
            "near",
            [base, listing, near_e, near_o],
            scratch=[pltpu.VMEM((2,) + listed, f32), pltpu.VMEM((m, 2 * agents), bf16),
                     pltpu.VMEM((2 * cy, 2 * agents), bf16)],
        )
        step = 4
        field, strips, strip_even, strip_odd, buffer, send = call(
            kernel(far_kernel, grid_count=grid_count, capacity=capacity, after=step),
            [(one_field, f32), ((4 * sweeps, 2 * m), f32), ((sweeps, 2 * m), f32), ((2 * sweeps, 2 * m), f32),
             ((species, columns), f32)] + [half_buffer],
            "far",
            [field, buffer, near_e, near_o, far_e, far_o],
            scratch=[pltpu.VMEM((2,) + listed, f32), pltpu.VMEM((head // 2, 2 * agents), bf16),
                     pltpu.VMEM((2 * cy, 2 * agents), bf16)],
        )
        got = swap(send, lambda g, h: (g ^ step, h))
        got_odd = swap(strip_odd, side_odd)
        got_even = swap(strip_even, side_even)
        (inside,) = call(
            kernel(sweep_kernel, grid_count=grid_count), [((nz, cx, cy), f32)], "sweeps", [field]
        )
        while step < grid_count // 2:
            after = 2 * step
            buffer, sent = call(
                kernel(relay_kernel, capacity=capacity, step=step, after=after),
                [((species, columns), f32), half_buffer],
                "relay",
                [buffer, got],
            )
            step = after
            got = swap(sent, lambda g, h: (g ^ step, h))
        tiles = 2 * m // LANES
        new_oxygen, daughter_state = call(
            kernel(strip_kernel, grid_count=grid_count, row_count=row_count, capacity=capacity, step=step),
            [((nz // tiles, tiles, cx, cy), f32), ((species, columns), f32)],
            "strips",
            [inside, strips, got_even, got_odd, buffer, got],
            hbm=(6, 7),
            scratch=[pltpu.VMEM((tiles, nz // tiles, cx, cy), f32), pltpu.VMEM((species, columns), f32),
                     pltpu.SemaphoreType.DMA((tiles + 1,))],
        )
        return new_state, daughter_state, new_oxygen.reshape(nz, cx, cy)

    return jax.shard_map(
        shards,
        mesh=mesh,
        in_specs=(
            P(None, GRID), P(), P(), P(), P(), P(), P(GRID), P(GRID), P(GRID, None), P(GRID), P(None, "gx", "gy"),
        ),
        out_specs=(P(None, GRID), P(None, GRID), P(None, "gx", "gy")),
        check_vma=False,
    )
```

```python
import jax
import jax.numpy as jnp
from jax import lax
from jax.experimental import pallas as pl
from jax.experimental.pallas import tpu as pltpu
from jax.sharding import PartitionSpec as P

time_step = 0.25
diffusion_number = 0.16
sweeps = 4
GRID = ("gx", "gy")
LANES = 128
EXACT = lax.Precision.HIGHEST
f32, bf16, i32 = jnp.float32, jnp.bfloat16, jnp.int32
VMEM_LIMIT = 48 << 20


def call(body, outs, name, inputs, smem=(), hbm=(), scratch=(), cost=None):
    def spec(at, shape):
        if at in smem:
            return pl.BlockSpec(memory_space=pltpu.SMEM)
        return pl.BlockSpec(memory_space=pltpu.HBM) if at in hbm else pl.BlockSpec(memory_space=pltpu.VMEM)

    count = len(inputs)
    inputs = [pltpu.with_memory_space_constraint(v, pltpu.HBM) if at in hbm else v for at, v in enumerate(inputs)]
    return pl.pallas_call(
        body,
        out_shape=tuple(jax.ShapeDtypeStruct(s, t) for s, t in outs),
        in_specs=[spec(at, value.shape) for at, value in enumerate(inputs)],
        out_specs=tuple(spec(count + at, s) for at, (s, t) in enumerate(outs)),
        scratch_shapes=scratch,
        compiler_params=pltpu.CompilerParams(vmem_limit_bytes=VMEM_LIMIT),
        name=name,
    )(*inputs)


def swap_pairs(grid_count, row_count, partner):
    pairs = []
    for g in range(grid_count):
        for h in range(row_count):
            p, q = partner(g, h)
            if not (0 <= p < grid_count and 0 <= q < row_count):
                p, q = g, h ^ 1
            pairs.append((g * row_count + h, p * row_count + q))
    return pairs


def near_even(g, h):
    return g ^ 1, h


def near_odd(g, h):
    return (g + 1 if g % 2 else g - 1), h


def far_even(g, h):
    return g ^ 2, h


def far_odd(g, h):
    return (g + 2 if g & 2 else g - 2), h


def side_even(g, h):
    return g, h ^ 1


def column(row, count):
    shape = (count, count)
    same = lax.broadcasted_iota(i32, shape, 0) == lax.broadcasted_iota(i32, shape, 1)
    return jnp.sum(jnp.where(same, jnp.broadcast_to(row, shape), 0), axis=1, keepdims=True)


def advance_kernel(
    count_ref, cell_hbm, coupling_hbm, basal_hbm, half_hbm, decay_hbm, weight_hbm, voxel_hbm, oxygen_hbm, ids_hbm,
    targets_hbm, new_state, message_even, message_odd, message_far, buffer,
    cell, coupling, basal, half, decay, weight, voxel, oxygen, ids, targets, drive, matrices, stack, chosen, codes, semaphores,
    *, cy, cx, nz, capacity,
):
    pairs = (
        (ids_hbm, ids), (voxel_hbm, voxel), (targets_hbm, targets), (coupling_hbm, coupling), (basal_hbm, basal),
        (half_hbm, half), (decay_hbm, decay), (weight_hbm, weight), (cell_hbm, cell), (oxygen_hbm, oxygen),
    )
    species, agents = cell.shape
    copies = [pltpu.make_async_copy(a, b, semaphores.at[i]) for i, (a, b) in enumerate(pairs)]
    for copy in copies:
        copy.start()
    stack[...] = jnp.zeros_like(stack)
    for copy in copies[:-2]:
        copy.wait()
    rows = agents // LANES
    picks = ids.shape[1]
    chosen[...] = (lax.broadcasted_iota(i32, (agents, picks), 0) == ids[...]).astype(f32).astype(bf16)
    code = voxel[...]
    at_y = code % cy
    at_x = (code // cy) % cx
    at_z = (code // (cy * cx)) % nz
    slab_x = (code // (cy * cx * nz)) * cx + at_x + cx // 2
    codes[:rows, :] = (at_z * cx + slab_x % cx - nz * cx // 2).astype(f32)
    codes[rows:, :] = ((slab_x // cx) * cy + at_y - 2 * cy).astype(f32)
    basal_c, half_c, decay_c, weight_c = (column(r[...], species) for r in (basal, half, decay, weight))
    half_square = half_c * half_c
    matrix_high, matrix_low, _ = pieces(coupling[...])
    matrices[...] = jnp.zeros_like(matrices)
    for number, piece in enumerate((matrix_high, matrix_high, matrix_low)):
        matrices[:, number * PIECE_ROWS : number * PIECE_ROWS + species] = piece
    matrix = matrices[...]

    def rates(current):
        square = current * current
        occupancy = square / (half_square + square)
        high = occupancy.astype(bf16)
        low = (occupancy - high.astype(f32)).astype(bf16)
        for number, piece in enumerate((high, low, high)):
            stack[number * PIECE_ROWS : number * PIECE_ROWS + species, :] = piece
        drive_sum = jnp.dot(matrix, stack[...], preferred_element_type=f32)
        return basal_c + drive_sum - decay_c * current

    placing = place_columns(targets[...], capacity, buffer.shape[1])
    copies[-2].wait()
    current = cell[...]
    for substep in range(2):
        middle = current + (0.5 * time_step) * rates(current)
        current = current + time_step * rates(middle)
    new_state[...] = current
    total = jnp.sum(weight_c * current, axis=0, keepdims=True)
    for c in range(rows):
        drive[c : c + 1, :] = total[:, c * LANES : (c + 1) * LANES]
    stacked = [jnp.pad(p, ((0, PIECE_ROWS - species), (0, 0))) for p in pieces(current)[:2]]
    both = jnp.dot(jnp.concatenate(stacked, axis=0), chosen[...], preferred_element_type=f32)
    mothers = both[:species] + both[PIECE_ROWS : PIECE_ROWS + species]
    copies[-1].wait()
    x = drive[...]
    soft = jnp.maximum(x, 0.0) + jnp.log1p(jnp.exp(-jnp.abs(x)))
    slot = lax.broadcasted_iota(i32, (rows, LANES), 0) * LANES + lax.broadcasted_iota(i32, (rows, LANES), 1)
    uptake = jnp.where(slot < count_ref[0], soft, 0.0)
    listing = jnp.concatenate([uptake, codes[...]], axis=0).astype(bf16)
    own = oxygen[...] - 1.0
    turned = pltpu.roll(own, cx // 2, 1)
    low = lax.broadcasted_iota(i32, (nz // 2, cx, cy), 1) < cx // 2
    a, b = own[: nz // 2], own[nz // 2 :]
    ta, tb = turned[: nz // 2], turned[nz // 2 :]
    upper = jnp.where(low, ta, b)
    lower = jnp.where(low, a, tb)
    even = lax.axis_index("gx") % 2 == 0
    to_next = upper.reshape(nz // 2 * cx, cy)
    to_previous = lower.reshape(nz // 2 * cx, cy)
    head = nz // 2 * cx
    message_even[:head, :] = jnp.where(even, to_next, to_previous).astype(bf16)
    message_odd[:head, :] = jnp.where(even, to_previous, to_next).astype(bf16)
    tail = head + 3 * rows
    message_even[head:tail, :] = listing
    message_odd[head:, :] = listing
    message_far[...] = listing
    placed = sum(product(p, placing) for p in pieces(mothers)[:2])
    buffer[...] = placed
    put_pieces(message_even, tail, first_send(placed, lax.axis_index("gx") % 2 == 1, capacity))


def one_hots(lists, which, first, m, base, width, left, right, slot):
    rows = lists.shape[1] // 3
    pack = 16
    row_at = (lax.broadcasted_iota(i32, (m, LANES), 0) + first).astype(f32).astype(bf16).reshape(m // pack, pack, LANES)
    col_at = (lax.broadcasted_iota(i32, (width, LANES), 0) + base).astype(f32).astype(bf16)
    col_at = col_at.reshape(width // pack, pack, LANES)
    one, zero = jnp.ones((), bf16), jnp.zeros((), bf16)

    def line(at):
        return jnp.broadcast_to(lists[which, at : at + 1, :], (pack, LANES)).astype(bf16)[None]

    for at in range(rows):
        columns = slice((slot * rows + at) * LANES, (slot * rows + at + 1) * LANES)
        hit = jnp.where(row_at == line(rows + at), one, zero)
        left[:, columns] = hit.reshape(m, LANES)
        spread = jnp.where(col_at == line(2 * rows + at), jnp.broadcast_to(line(at), col_at.shape), zero)
        right[:width, columns] = spread.reshape(width, LANES)


def product(left, right):
    return lax.dot_general(left, right, (((1,), (1,)), ((), ())), preferred_element_type=f32)


def own_kernel(oxygen_hbm, own_list, state, base, new_state, lists, left, right, oxygen, semaphores):
    copy = pltpu.make_async_copy(oxygen_hbm, oxygen, semaphores.at[0])
    copy.start()
    store = pltpu.make_async_copy(state, new_state, semaphores.at[1])
    store.start()
    nz, cx, cy = oxygen.shape
    m = nz * cx
    lists[0] = own_list[...].astype(f32)
    one_hots(lists, 0, -m // 2, m, -cy, 2 * cy, left, right, 0)
    total = product(left[...], right[...])
    copy.wait()
    low = lax.broadcasted_iota(i32, (nz, cx, cy), 1) < cx // 2
    inner = pltpu.roll(oxygen[...], cx // 2, 1)
    base[:, :cx, :] = jnp.where(low, 0.0, inner) - total[:, :cy].reshape(nz, cx, cy)
    base[:, cx:, :] = jnp.where(low, inner, 0.0) - total[:, cy:].reshape(nz, cx, cy)
    store.wait()


def keep(listing, rows, valid):
    index = lax.broadcasted_iota(i32, listing.shape, 0)
    return jnp.where((index < rows) & jnp.logical_not(valid), 0.0, listing)


def relay_first_kernel(buffer, got, listing, merged, message, *, capacity, head):
    g = lax.axis_index("gx")
    species = buffer.shape[0]
    count = listing.shape[0]
    value = take_in(buffer[...], get_pieces(got, head + count, species), g % 2 == 1, capacity)
    merged[...] = value
    message[:count, :] = listing[...]
    put_pieces(message, count, first_send(value, (g // 2) % 2 == 1, 2 * capacity))


def near_kernel(base, listing, near_e, near_o, field, lists, left, right, *, grid_count):
    nz, cx, cy = base.shape[0], base.shape[1] // 2, base.shape[2]
    m, head = nz * cx, nz // 2 * cx
    count = listing.shape[0]
    rows = count // 3
    g = lax.axis_index("gx")
    even = g % 2 == 0
    e, o = near_e[head : head + count, :].astype(f32), near_o[head : head + count, :].astype(f32)
    lists[0] = keep(jnp.where(even, e, o), rows, g + 1 < grid_count)
    lists[1] = keep(jnp.where(even, o, e), rows, g >= 1)
    one_hots(lists, 0, -m // 2, m, -2 * cy, 2 * cy, left, right, 0)
    one_hots(lists, 1, -m // 2, m, 0, 2 * cy, left, right, 1)
    total = product(left[...], right[...])
    field[:, :cx, :] = base[:, :cx, :] - total[:, :cy].reshape(nz, cx, cy)
    field[:, cx:, :] = base[:, cx:, :] - total[:, cy:].reshape(nz, cx, cy)


def far_kernel(
    base, buffer, near_e, near_o, far_e, far_o, field, strips, strip_even, strip_odd, merged, send,
    lists, left, right, *, grid_count, capacity, after,
):
    nz, cx, cy = base.shape[0], base.shape[1] // 2, base.shape[2]
    half, zh = cx // 2, nz // 2
    head, m = zh * cx, nz * cx
    count = far_o.shape[0]
    rows = count // 3
    agents = rows * LANES
    g = lax.axis_index("gx")
    even = g % 2 == 0
    low_pair = g % 4 < 2
    fe, fo = far_e[:count, :].astype(f32), far_o[...].astype(f32)
    quarter = zh // 2
    for which, listing, base_code, valid in (
        (0, jnp.where(low_pair, fe, fo), -2 * cy, g + 2 < grid_count),
        (1, jnp.where(low_pair, fo, fe), cy, g >= 2),
    ):
        code = listing[rows : 2 * rows].astype(i32) + m // 2
        at_z, at_y = code // cx, listing[2 * rows :].astype(i32) - base_code
        inner_z = at_z % zh
        code = (inner_z % quarter) * cx + (inner_z // quarter) * half + code % half
        lists[which, :rows] = jnp.where(valid, listing[:rows], 0.0)
        lists[which, rows : 2 * rows] = code.astype(f32)
        lists[which, 2 * rows :] = jnp.where((at_y >= 0) & (at_y < cy), (at_z // zh) * cy + at_y, -1).astype(f32)
    one_hots(lists, 0, 0, head // 2, 0, 2 * cy, left, right, 0)
    one_hots(lists, 1, 0, head // 2, 0, 2 * cy, left, right, 1)
    low_quarter = lax.broadcasted_iota(i32, (quarter, cx, cy), 1) < half

    def unfold(total):
        lower, upper = (total[:, t * cy : (t + 1) * cy].reshape(quarter, cx, cy) for t in range(2))
        return jnp.concatenate(
            [
                jnp.where(low_quarter, lower, pltpu.roll(upper, half, 1)),
                jnp.where(low_quarter, pltpu.roll(lower, half, 1), upper),
            ],
            axis=0,
        )

    past_after = unfold(product(left[:, :agents], right[:, :agents]))
    past_before = unfold(product(left[:, agents:], right[:, agents:]))

    e, o = near_e[:head, :].astype(f32), near_o[:head, :].astype(f32)
    shape = (zh, cx, cy)
    from_before = jnp.where(g >= 1, jnp.where(even, o, e) + 1.0, 0.0).reshape(shape) - past_before
    from_after = jnp.where(g + 1 < grid_count, jnp.where(even, e, o) + 1.0, 0.0).reshape(shape) - past_after
    low = lax.broadcasted_iota(i32, shape, 1) < half
    field[:zh, :cx] = base[:zh, :cx] + jnp.where(low, from_before, 0.0)
    field[zh:, :cx] = base[zh:, :cx] + jnp.where(low, pltpu.roll(from_before, half, 1), 0.0)
    field[:zh, cx:] = base[:zh, cx:] + jnp.where(low, 0.0, pltpu.roll(from_after, half, 1))
    field[zh:, cx:] = base[zh:, cx:] + jnp.where(low, 0.0, from_after)

    edge = 2 * sweeps
    picked = lax.broadcasted_iota(i32, (2 * edge, cy), 0)
    picked = jnp.where(picked < edge, picked, picked + cy - 2 * edge)
    picker = (picked == lax.broadcasted_iota(i32, (2 * edge, cy), 1)).astype(f32).astype(bf16)
    tiles = 2 * m // LANES
    value = field[...].reshape(nz // tiles, tiles, 2 * cx, cy)
    flat = jnp.concatenate([value[:, k].reshape(LANES, cy) for k in range(tiles)], axis=0)
    rims = product(jnp.concatenate([picker, picker], axis=1), jnp.concatenate(pieces(flat)[:2], axis=1))
    strips[...] = rims
    h_even = lax.axis_index("gy") % 2 == 0
    head_rows, tail_rows = rims[:sweeps], rims[2 * edge - sweeps :]
    strip_even[...] = jnp.where(h_even, tail_rows, head_rows)
    strip_odd[:sweeps, :] = jnp.where(h_even, head_rows, tail_rows)
    strip_odd[sweeps:, :] = head_rows
    value = take_in(buffer[...], get_pieces(far_e, count, buffer.shape[0]), (g // 2) % 2 == 1, 2 * capacity)
    merged[...] = value
    send[...] = first_send(value, (g // after) % 2 == 1, after * capacity)


def sweep_kernel(field, out, *, grid_count):
    nz, width, cy = field.shape
    half = width // 4
    g = lax.axis_index("gx")
    at_x = lax.broadcasted_iota(i32, (nz, width, cy), 1)
    outside = (g == 0) & (at_x < half) | (g == grid_count - 1) & (at_x >= width - half)
    scale = jnp.where(outside, 0.0, diffusion_number)
    centre = 1.0 / diffusion_number - 6.0
    plane = jnp.zeros((1, width, cy), f32)
    value = field[...]
    for turn in range(sweeps):
        total = jnp.concatenate([plane, value[:-1]], axis=0) + jnp.concatenate([value[1:], plane], axis=0)
        total = total + (pltpu.roll(value, 1, 1) + pltpu.roll(value, width - 1, 1))
        total = total + (pltpu.roll(value, 1, 2) + pltpu.roll(value, cy - 1, 2))
        value = (total + centre * value) * scale
    low = lax.broadcasted_iota(i32, (nz, width // 2, cy), 1) < half
    out[...] = pltpu.roll(jnp.where(low, value[:, width // 2 :], value[:, : width // 2]), half, 1)


def strip_kernel(
    inside, strips, got_even, got_odd, buffer, got, out, daughters, merged, taken, semaphores,
    *, grid_count, row_count, capacity, step,
):
    taken[...] = take_in(
        buffer[...], got[...], (lax.axis_index("gx") // step) % 2 == 1, capacity * step
    )
    copies = [pltpu.make_async_copy(taken, daughters, semaphores.at[0])]
    copies[0].start()
    nz, cx, cy = inside.shape
    m = strips.shape[1]
    width = m // nz
    g, h = lax.axis_index("gx"), lax.axis_index("gy")
    h_even = h % 2 == 0
    edge = 2 * sweeps
    has_right, has_left = h + 1 < row_count, h >= 1
    a, b = got_even[...], got_odd[:sweeps, :]
    right = jnp.where(has_right, jnp.where(h_even, a, b), 0.0)
    left = jnp.where(has_left, jnp.where(h_even, b, a), 0.0)
    own = strips[...]
    tiles = m // LANES
    bands = [
        jnp.concatenate([rows[:, k * LANES : (k + 1) * LANES] for rows in (left, own, right)], axis=0) for k in range(tiles)
    ]
    shape = bands[0].shape
    count = shape[0]
    lane = lax.broadcasted_iota(i32, shape, 1)
    line = lax.broadcasted_iota(i32, shape, 0)
    outside = (line < sweeps) & jnp.logical_not(has_left) | (line >= count - sweeps) & jnp.logical_not(has_right)
    at_x = lane % width
    outside = outside | (g == 0) & (at_x < cx // 2) | (g == grid_count - 1) & (at_x >= width - cx // 2)
    scale = jnp.where(outside, 0.0, diffusion_number)
    z_first, z_last = lane < width, lane >= LANES - width
    centre = 1.0 / diffusion_number - 6.0
    for turn in range(sweeps):
        wrapped = jnp.where(z_first, 0.0, pltpu.roll(bands[-1], width, 1))
        onward = jnp.where(z_last, 0.0, pltpu.roll(bands[0], LANES - width, 1))
        around = [wrapped] + bands + [onward]
        bands = [
            (
                (around[k] + around[k + 2])
                + (pltpu.roll(b, 1, 0) + pltpu.roll(b, count - 1, 0))
                + (pltpu.roll(b, 1, 1) + pltpu.roll(b, LANES - 1, 1))
                + centre * b
            ) * scale
            for k, b in enumerate(bands)
        ]
    placed = lax.broadcasted_iota(i32, (edge, cy), 0)
    placed = jnp.where(placed < sweeps, placed, placed + cy - edge)
    placer = (placed == lax.broadcasted_iota(i32, (edge, cy), 1)).astype(f32)
    placers = jnp.concatenate([placer, placer], axis=0).astype(bf16)
    planes = nz // tiles
    low = lax.broadcasted_iota(i32, (planes, cx, cy), 1) < cx // 2
    at_y = lax.broadcasted_iota(i32, (planes, cx, cy), 2)
    rim = (at_y < sweeps) | (at_y >= cy - sweeps)
    for k, b in enumerate(bands):
        final = jnp.concatenate([b[sweeps : 2 * sweeps], b[count - 2 * sweeps : count - sweeps]], axis=0)
        high = final.astype(bf16).astype(f32)
        stacked = jnp.concatenate([high, final - high], axis=0).astype(bf16)
        edges = lax.dot_general(
            stacked, placers, (((0,), (0,)), ((), ())), preferred_element_type=f32
        ).reshape(planes, width, cy)
        mixed = pltpu.roll(jnp.where(low, edges[:, cx:], edges[:, :cx]), cx // 2, 1)
        for at in range(planes):
            z = at * tiles + k
            merged[k, at] = jnp.where(rim[at], mixed[at], inside[z])
        copies.append(pltpu.make_async_copy(merged.at[k], out.at[:, k], semaphores.at[k + 1]))
        copies[-1].start()
    for copy in copies:
        copy.wait()


def pieces(value):
    high = value.astype(bf16)
    rest = value - high.astype(f32)
    middle = rest.astype(bf16)
    return high, middle, (rest - middle.astype(f32)).astype(bf16)


PIECE_ROWS = 48


def put_pieces(message, at, value):
    for number, piece in enumerate(pieces(value)[:2]):
        start = at + number * PIECE_ROWS
        message[start : start + value.shape[0], :] = piece


def get_pieces(message, at, count):
    starts = [at + number * PIECE_ROWS for number in range(2)]
    return sum(message[start : start + count, :].astype(f32) for start in starts)


def first_send(buffer, mine, width):
    count = buffer.shape[1]
    half = count // 2
    left, right = buffer[:, :half], buffer[:, half:]
    if width == half:
        return jnp.where(mine, left, right)
    bit = (lax.broadcasted_iota(i32, left.shape, 1) // width) % 2 == 1
    moved = jnp.where(mine, pltpu.roll(right, width, 1), pltpu.roll(right, half - width, 1))
    return jnp.where(jnp.logical_xor(bit, mine), left, moved)


def take_in(buffer, got, mine, width):
    count = buffer.shape[1]
    half = count // 2
    left, right = buffer[:, :half], buffer[:, half:]
    if width == half:
        left, right = jnp.where(mine, got, left), jnp.where(mine, right, got)
    else:
        bit = (lax.broadcasted_iota(i32, left.shape, 1) // width) % 2 == 1
        other = jnp.logical_xor(bit, mine)
        moved = jnp.where(mine, pltpu.roll(got, half - width, 1), pltpu.roll(got, width, 1))
        left, right = jnp.where(other, moved, left), jnp.where(other, got, right)
    return jnp.concatenate([left, right], axis=1)


def place_columns(target, capacity, columns):
    picks = target.shape[1]
    square = (picks, picks)
    across = jnp.broadcast_to(target, square)
    down = jnp.broadcast_to(column(target, picks), square)
    earlier = lax.broadcasted_iota(i32, square, 0) < lax.broadcasted_iota(i32, square, 1)
    rank = jnp.sum(jnp.where((across == down) & earlier, 1, 0), axis=0, keepdims=True)
    position = target * capacity + rank
    return (lax.broadcasted_iota(i32, (columns, picks), 0) == position).astype(f32).astype(bf16)


def relay_kernel(buffer, got, merged, send, *, capacity, step, after):
    g = lax.axis_index("gx")
    value = take_in(buffer[...], got[...], (g // step) % 2 == 1, capacity * step)
    merged[...] = value
    send[...] = first_send(value, (g // after) % 2 == 1, capacity * after)


def solution(mesh):
    grid_count, row_count = mesh.shape["gx"], mesh.shape["gy"]

    def swap(value, partner):
        return lax.ppermute(value, GRID, swap_pairs(grid_count, row_count, partner))

    def side_odd(g, h):
        p = h + 1 if h % 2 else h - 1
        return (g, p) if 0 <= p < row_count else (g, h ^ (row_count - 1))

    def shards(
        cell_state, coupling, basal_rate, half_sat, decay_rate, uptake_weight,
        agent_counts, divider_ids, destinations, voxel_index, oxygen,
    ):
        species, agents = cell_state.shape
        nz, cx, cy = oxygen.shape
        picks = divider_ids.shape[0]
        rows = agents // LANES
        head = nz // 2 * cx
        capacity = max(2, 2 * picks // grid_count)
        columns = grid_count * capacity

        def line(value):
            return value.reshape(1, -1)

        def kernel(body, **sizes):
            def run(*refs):
                return body(*refs, **sizes)

            return run

        m = nz * cx
        count = 3 * rows
        pieces_rows = 2 * PIECE_ROWS
        one_field = (nz, 2 * cx, cy)
        listed = (count, LANES)
        half_buffer = ((species, columns // 2), f32)
        assert species <= PIECE_ROWS and columns == 2 * LANES and grid_count >= 8

        state, message_even, message_odd, listing, buffer = call(
            kernel(advance_kernel, cy=cy, cx=cx, nz=nz, capacity=capacity),
            [((species, agents), f32), ((head + count + pieces_rows, LANES), bf16), ((head + count, LANES), bf16),
             (listed, bf16), ((species, columns), f32)],
            "advance",
            [agent_counts, cell_state, coupling, line(basal_rate), line(half_sat), line(decay_rate),
             line(uptake_weight), voxel_index.reshape(rows, LANES), oxygen, line(divider_ids), line(destinations)],
            smem=(0,),
            hbm=range(1, 11),
            scratch=[pltpu.VMEM((species, agents), f32), pltpu.VMEM((species, species), f32)]
            + [pltpu.VMEM((1, species), f32)] * 4
            + [pltpu.VMEM((rows, LANES), i32), pltpu.VMEM((nz, cx, cy), f32)]
            + [pltpu.VMEM((1, picks), i32)] * 2
            + [pltpu.VMEM((rows, LANES), f32), pltpu.VMEM((species, 3 * PIECE_ROWS), bf16),
               pltpu.VMEM((3 * PIECE_ROWS, agents), bf16), pltpu.VMEM((agents, picks), bf16),
               pltpu.VMEM((2 * rows, LANES), f32), pltpu.SemaphoreType.DMA((10,))],
        )
        near_e = swap(message_even, near_even)
        near_o = swap(message_odd, near_odd)
        base, new_state = call(
            own_kernel,
            [(one_field, f32), ((species, agents), f32)],
            "own",
            [oxygen, listing, state],
            hbm=(0, 4),
            scratch=[pltpu.VMEM((1,) + listed, f32), pltpu.VMEM((m, agents), bf16), pltpu.VMEM((2 * cy, agents), bf16),
                     pltpu.VMEM((nz, cx, cy), f32), pltpu.SemaphoreType.DMA((2,))],
        )
        buffer, base = lax.optimization_barrier((buffer, base))
        buffer, message_far = call(
            kernel(relay_first_kernel, capacity=capacity, head=head),
            [((species, columns), f32), ((count + pieces_rows, LANES), bf16)],
            "relay",
            [buffer, near_e, listing],
        )
        far_e = swap(message_far, far_even)
        far_o = swap(listing, far_odd)
        base, _ = lax.optimization_barrier((base, message_far))
        (field,) = call(
            kernel(near_kernel, grid_count=grid_count),
            [(one_field, f32)],
            "near",
            [base, listing, near_e, near_o],
            scratch=[pltpu.VMEM((2,) + listed, f32), pltpu.VMEM((m, 2 * agents), bf16),
                     pltpu.VMEM((2 * cy, 2 * agents), bf16)],
        )
        step = 4
        field, strips, strip_even, strip_odd, buffer, send = call(
            kernel(far_kernel, grid_count=grid_count, capacity=capacity, after=step),
            [(one_field, f32), ((4 * sweeps, 2 * m), f32), ((sweeps, 2 * m), f32), ((2 * sweeps, 2 * m), f32),
             ((species, columns), f32)] + [half_buffer],
            "far",
            [field, buffer, near_e, near_o, far_e, far_o],
            scratch=[pltpu.VMEM((2,) + listed, f32), pltpu.VMEM((head // 2, 2 * agents), bf16),
                     pltpu.VMEM((2 * cy, 2 * agents), bf16)],
        )
        got = swap(send, lambda g, h: (g ^ step, h))
        got_odd = swap(strip_odd, side_odd)
        got_even = swap(strip_even, side_even)
        (inside,) = call(
            kernel(sweep_kernel, grid_count=grid_count), [((nz, cx, cy), f32)], "sweeps", [field]
        )
        while step < grid_count // 2:
            after = 2 * step
            buffer, sent = call(
                kernel(relay_kernel, capacity=capacity, step=step, after=after),
                [((species, columns), f32), half_buffer],
                "relay",
                [buffer, got],
            )
            step = after
            got = swap(sent, lambda g, h: (g ^ step, h))
        tiles = 2 * m // LANES
        new_oxygen, daughter_state = call(
            kernel(strip_kernel, grid_count=grid_count, row_count=row_count, capacity=capacity, step=step),
            [((nz // tiles, tiles, cx, cy), f32), ((species, columns), f32)],
            "strips",
            [inside, strips, got_even, got_odd, buffer, got],
            hbm=(6, 7),
            scratch=[pltpu.VMEM((tiles, nz // tiles, cx, cy), f32), pltpu.VMEM((species, columns), f32),
                     pltpu.SemaphoreType.DMA((tiles + 1,))],
        )
        return new_state, daughter_state, new_oxygen.reshape(nz, cx, cy)

    return jax.shard_map(
        shards,
        mesh=mesh,
        in_specs=(
            P(None, GRID), P(), P(), P(), P(), P(), P(GRID), P(GRID), P(GRID, None), P(GRID), P(None, "gx", "gy"),
        ),
        out_specs=(P(None, GRID), P(None, GRID), P(None, "gx", "gy")),
        check_vma=False,
    )
```
